32 devices in a mesh: azim: 8 (over y, x, core), radax: 4 (over z).
Axes of the slice: x: 2, y: 2, z: 4, core: 2. Of those that a mesh axis runs over, the one named last changes fastest.
Arguments:
- gas: float32 [14, 32, 128, 128], P(None, 'azim', 'radax'), may hold values from -6 to 6
- transport: float32 [3, 14], replicated, may hold values from 0.02 to 0.12
- chemistry: float32 [14, 14], replicated, may hold values from -1.2 to 1.2
- evap_weight: float32 [14], replicated, may hold values from -1.5 to 1.5
- source_map: float32 [14, 8], replicated, may hold values from -2 to 2
- parcel_mass: float32 [8, 4, 2048], P('azim', 'radax'), may hold values from 0.2 to 2
- parcel_state: float32 [7, 8, 4, 2048], P(None, 'azim', 'radax'), may hold values from -6 to 6
- parcel_host: int32 [8, 4, 2048], P('azim', 'radax'), may hold values from 0 to 16383
- parcel_count: int32 [8, 4], P('azim', 'radax'), may hold values from 384 to 1536, as said below
- crossing: int32 [8, 4, 2, 2, 128], P('azim', 'radax'), may hold values from 0 to 2048, as said below
Outputs:
- gas_next: float32 [14, 32, 128, 128], P(None, 'azim', 'radax')
- mass_next: float32 [8, 4, 2048], P('azim', 'radax')
- state_next: float32 [7, 8, 4, 2048], P(None, 'azim', 'radax')
- host_next: int32 [8, 4, 2048], P('azim', 'radax')
- count_next: int32 [8, 4], P('azim', 'radax')
The draws below stay inside these ranges and needn't reach their ends.
Inputs may be any that keep to these rules, and one draw needn't show every extreme that they name: `parcel_count`: every device's count lies in 1536 halved zero, one or two times; some device holds exactly 1536. `crossing`: each list holds 64 to 128 distinct ascending slots below 2048, then the value 2048; the four lists of a device are disjoint. In every draw a list of each section and direction is full on some device, and some device with the largest count receives full lists from both neighbours in both sections.
All inputs are finite; a program needn't handle non-finite values.
Results may differ from the reference program's by a relative error of at most 0.0009.
Values sent between devices are 32-bit elements; how exact they have to be, the bound alone decides.
No kernel may reach another device: no remote copies, remote signals or barrier semaphores. Data moves between devices by JAX's collectives and lax.ppermute only.
A program may use at most 64 MiB of HBM per device.

```python
import math
from functools import partial
import jax
import jax.numpy as jnp
from jax import lax

F = 14
STATE = 7
CA = 4
CR = 32
CZ = 128
P_SIZE = 2048
M = 128
NA = 32
NR = 128
N_AZIM = 8
N_RADAX = 4


def plan_parcels(key):
    spare = P_SIZE - 4 * M
    k_level, k_azim, k_radax, k_sizes, k_force, k_order = jax.random.split(jax.random.fold_in(key, 7), 6)
    azim_ids = jnp.arange(N_AZIM, dtype=jnp.int32)[:, None]
    radax_ids = jnp.arange(N_RADAX, dtype=jnp.int32)[None, :]
    star_azim = jax.random.randint(k_azim, (), 0, N_AZIM)
    star_radax = jax.random.randint(k_radax, (), 0, N_RADAX)
    is_star = (azim_ids == star_azim) & (radax_ids == star_radax)
    level = jax.random.randint(k_level, (N_AZIM, N_RADAX), 0, 3)
    level = jnp.where(is_star, 0, level)
    count = jnp.where(level == 0, spare, jnp.where(level == 1, spare // 2, spare // 4)).astype(jnp.int32)
    sizes = jax.random.randint(k_sizes, (N_AZIM, N_RADAX, 2, 2), M // 2, M + 1)
    device_ids = (azim_ids * N_RADAX + radax_ids)[:, :, None, None]
    forced = jax.random.randint(k_force, (2, 2), 0, N_AZIM * N_RADAX)
    sizes = jnp.where(device_ids == forced[None, None], M, sizes)
    dir_ids = jnp.arange(2, dtype=jnp.int32)[None, None, None, :]
    left_side = ((azim_ids == (star_azim - 1) % N_AZIM) & (radax_ids == star_radax))[:, :, None, None]
    right_side = ((azim_ids == (star_azim + 1) % N_AZIM) & (radax_ids == star_radax))[:, :, None, None]
    sizes = jnp.where(left_side & (dir_ids == 1), M, sizes)
    sizes = jnp.where(right_side & (dir_ids == 0), M, sizes)
    keys = jax.random.split(k_order, N_AZIM * N_RADAX)
    ranks = jax.vmap(lambda one: jax.random.permutation(one, P_SIZE))(keys).reshape(N_AZIM, N_RADAX, P_SIZE).astype(jnp.int32)
    slot_ids = jnp.arange(P_SIZE, dtype=jnp.int32)[None, None, :]
    score = jnp.where(slot_ids < count[:, :, None], ranks, ranks + P_SIZE)
    order = jnp.argsort(score, axis=-1, stable=True)[:, :, :4 * M].reshape(N_AZIM, N_RADAX, 2, 2, M).astype(jnp.int32)
    position = jnp.arange(M, dtype=jnp.int32)
    lists = jnp.where(position < sizes[..., None], order, P_SIZE)
    lists = jnp.sort(lists, axis=-1).astype(jnp.int32)
    return (count, lists)


def draw_parcel_count(key, part):
    return plan_parcels(key)[0]


def draw_crossing(key, part):
    return plan_parcels(key)[1]


def plant(drawn, key, low, top_value):
    longest = drawn.shape.index(max(drawn.shape))
    spots = []
    for shift in (0, 1):
        where = [jax.random.randint(jax.random.fold_in(key, axis), (), 0, length) for axis, length in enumerate(drawn.shape)]
        where[longest] = (where[longest] + shift) % drawn.shape[longest]
        spots.append(tuple(where))
    return drawn.at[spots[0]].set(low).at[spots[1]].set(top_value)


def shard_levels(own_key, extent, pieces, least, high):
    def one(axis_at, blocks):
        heights = jax.random.uniform(jax.random.fold_in(jax.random.fold_in(own_key, 6), axis_at), (blocks,), jnp.float32, least / len(pieces), high / len(pieces))
        return jnp.repeat(jnp.exp(heights), extent[axis_at] // blocks).reshape((-1,) + (1,) * (len(extent) - axis_at - 1))

    level = one(*pieces[0])
    for cut in pieces[1:]:
        level = level * one(*cut)
    return level


def noise(own_key, dims, deviation, reach, shards=(), held_as=jnp.bfloat16):
    gain = shard_levels(own_key, dims, shards, -0.22, 0.18) if shards else 1.0
    values = jax.random.normal(own_key, dims, jnp.float32) * deviation * gain
    return jnp.minimum(jnp.maximum(values, -reach), reach).astype(held_as)


def setup_inputs(seed: int = 0) -> dict:
    arg_keys = jax.random.split(jax.random.key(seed), 11)
    gas = noise(arg_keys[0], (F, NA, NR, CZ), 1.0, 6.0, ((1, 8), (2, 4)), jnp.float32)
    transport = jnp.clip(jax.random.uniform(arg_keys[1], (3, F), jnp.float32, 0.02, 0.12), 0.02, 0.12)
    chemistry = noise(arg_keys[2], (F, F), 0.2, 1.2, (), jnp.float32)
    evap_weight = noise(arg_keys[3], (F,), F ** -0.5, 1.5, (), jnp.float32)
    source_map = noise(arg_keys[4], (F, STATE + 1), (STATE + 1) ** -0.5, 2.0, (), jnp.float32)
    parcel_mass = jnp.clip(jnp.exp(math.log(2.0) - 2.3025851 * jax.random.uniform(arg_keys[5], (N_AZIM, N_RADAX, P_SIZE), jnp.float32) ** shard_levels(arg_keys[5], (N_AZIM, N_RADAX, P_SIZE), ((0, 8), (1, 4)), -0.2, 0.2)), 0.2, 2.0)
    parcel_state = noise(arg_keys[6], (STATE, N_AZIM, N_RADAX, P_SIZE), 1.0, 6.0, ((1, 8), (2, 4)), jnp.float32)
    parcel_host = plant(jax.random.randint(arg_keys[7], (N_AZIM, N_RADAX, P_SIZE), 0, CA * CR * CZ), jax.random.fold_in(arg_keys[7], 1), 0, (CA * CR * CZ) - 1).astype(jnp.int32)
    parcel_count = draw_parcel_count(jax.random.fold_in(arg_keys[10], 71), 0)
    crossing = draw_crossing(jax.random.fold_in(arg_keys[10], 71), 0)
    return dict(gas=gas, transport=transport, chemistry=chemistry, evap_weight=evap_weight, source_map=source_map, parcel_mass=parcel_mass, parcel_state=parcel_state, parcel_host=parcel_host, parcel_count=parcel_count, crossing=crossing)


HIGH = lax.Precision.HIGHEST
DT = 0.5
RELAX = 0.3
EVAP = 0.5


def spatial_rhs(field, transport, chemistry):
    east = jnp.roll(field, -1, axis=1)
    west = jnp.roll(field, 1, axis=1)
    radial_pad = jnp.pad(field, ((0, 0), (0, 0), (1, 1), (0, 0)))
    north = radial_pad[:, :, 2:, :]
    south = radial_pad[:, :, :-2, :]
    axial_pad = jnp.pad(field, ((0, 0), (0, 0), (0, 0), (1, 1)))
    upper = axial_pad[..., 2:]
    lower = axial_pad[..., :-2]
    lap = east + west + north + south + upper + lower - 6.0 * field
    diffuse = transport[0][:, None, None, None]
    swirl = transport[1][:, None, None, None]
    axial = transport[2][:, None, None, None]
    chem = jnp.einsum("fg,gabz->fabz", chemistry, jnp.tanh(field), precision=HIGH)
    return diffuse * lap - swirl * 0.5 * (east - west) - axial * 0.5 * (upper - lower) + chem


def to_blocks(field):
    width = field.shape[0]
    split = field.reshape(width, N_AZIM, CA, N_RADAX, CR, CZ).transpose(1, 3, 0, 2, 4, 5)
    return split.reshape(N_AZIM, N_RADAX, width, CA * CR * CZ)


def from_blocks(blocks):
    width = blocks.shape[2]
    split = blocks.reshape(N_AZIM, N_RADAX, width, CA, CR, CZ).transpose(2, 0, 3, 1, 4, 5)
    return split.reshape(width, N_AZIM * CA, N_RADAX * CR, CZ)


def parcel_physics(flat, mass, state, host, live, evap_weight, source_map):
    probe = jnp.take(flat, host, axis=1)
    sig = jax.nn.sigmoid(jnp.dot(evap_weight, probe, precision=HIGH) + state[0])
    mdot = EVAP * mass * sig * live
    attr = jnp.concatenate([mass[None], state], axis=0)
    source = jnp.dot(source_map, attr, precision=HIGH) * mdot
    deposit = jnp.zeros_like(flat).at[:, host].add(source)
    new_mass = mass - DT * mdot
    temper = state[0:1] + DT * RELAX * (probe[4:5] - state[0:1])
    speeds = state[1:4] + DT * RELAX * (probe[1:4] - state[1:4])
    new_state = jnp.concatenate([temper, speeds, state[4:]], axis=0)
    return deposit, new_mass, new_state


def depart(mass, state, host, live, lists, span):
    slots = mass.shape[0]
    valid = lists < slots
    safe = jnp.where(valid, lists, 0)
    attr = jnp.concatenate([mass[None], state], axis=0)
    block = jnp.take(attr, safe, axis=1) * valid.astype(jnp.float32)
    host_row = jnp.where(valid, jnp.take(host, safe) % span, -1).astype(jnp.float32)
    packed = jnp.concatenate([block, host_row[None]], axis=0)
    live = live.at[lists.reshape(-1)].set(0.0, mode="drop")
    return packed[:, 1], packed[:, 0], live


def place(attr, host, live, packed, start, offset):
    slots = attr.shape[1]
    cells = packed[-1].astype(jnp.int32)
    valid = cells >= 0
    pos = jnp.where(valid, start + jnp.arange(cells.shape[0], dtype=jnp.int32), slots)
    attr = attr.at[:, pos].set(packed[:-1], mode="drop")
    host = host.at[pos].set(cells + offset, mode="drop")
    live = live.at[pos].set(1.0, mode="drop")
    return attr, host, live, jnp.sum(valid.astype(jnp.int32))


def arrive(mass, state, host, live, count, from_left, from_right, far_offset):
    attr = jnp.concatenate([mass[None], state], axis=0)
    attr, host, live, left_count = place(attr, host, live, from_left, count, 0)
    attr, host, live, right_count = place(attr, host, live, from_right, count + left_count, far_offset)
    return attr[0], attr[1:], host, live, count + left_count + right_count


def reference(gas, transport, chemistry, evap_weight, source_map, parcel_mass, parcel_state, parcel_host, parcel_count, crossing):
    span = CR * CZ
    far_offset = (CA - 1) * span
    physics = jax.vmap(jax.vmap(parcel_physics, in_axes=(0, 0, 0, 0, 0, None, None)), in_axes=(0, 0, 0, 0, 0, None, None))
    leave = jax.vmap(jax.vmap(partial(depart, span=span)))
    enter = jax.vmap(jax.vmap(partial(arrive, far_offset=far_offset)))
    mass = parcel_mass
    state = jnp.moveaxis(parcel_state, 0, 2)
    host = parcel_host
    count = parcel_count
    live = (jnp.arange(P_SIZE, dtype=jnp.int32)[None, None, :] < count[:, :, None]).astype(jnp.float32)

    def migrate(mass, state, host, live, count, section):
        right_going, left_going, live = leave(mass, state, host, live, crossing[:, :, section])
        from_left = jnp.roll(right_going, 1, axis=0)
        from_right = jnp.roll(left_going, -1, axis=0)
        return enter(mass, state, host, live, count, from_left, from_right)

    deposit, mass, state = physics(to_blocks(gas), mass, state, host, live, evap_weight, source_map)
    section_one = gas + DT * (spatial_rhs(gas, transport, chemistry) + from_blocks(deposit))
    mass, state, host, live, count = migrate(mass, state, host, live, count, 0)
    deposit, mass, state = physics(to_blocks(section_one), mass, state, host, live, evap_weight, source_map)
    gas_next = 0.5 * (gas + section_one + DT * (spatial_rhs(section_one, transport, chemistry) + from_blocks(deposit)))
    mass, state, host, live, count = migrate(mass, state, host, live, count, 1)
    mass_next = mass * live
    state_next = jnp.moveaxis(state * live[:, :, None, :], 2, 0)
    host_next = jnp.where(live > 0.5, host, -1)
    return gas_next, mass_next, state_next, host_next, count
```

```python
import functools

import jax
import jax.numpy as jnp
from jax import lax
from jax.experimental import pallas as pl
from jax.experimental.pallas import tpu as pltpu
from jax.sharding import PartitionSpec as P

DT = 0.5
RELAX = 0.3
EVAP = 0.5
F32 = jnp.float32
BF16 = jnp.bfloat16
ROWS = 16
HOST = 8
LIVE = 9
LANES = 128
LIMIT = 40 << 20

VMEM = pl.BlockSpec(memory_space=pltpu.VMEM)
SMEM = pl.BlockSpec(memory_space=pltpu.SMEM)
ANY = pl.BlockSpec(memory_space=pl.ANY)


def iota(shape, dim, dtype=jnp.int32):
    return lax.broadcasted_iota(dtype, shape, dim)


def parts_of(values, count):
    parts = []
    for _ in range(count - 1):
        part = values.astype(BF16)
        parts.append(part)
        values = values - part.astype(F32)
    return parts + [values.astype(BF16)]


def hot(mask):
    return mask.astype(F32).astype(BF16)


def across(left, right):
    return lax.dot_general(left, right, (((1,), (1,)), ((), ())), preferred_element_type=F32)


def call(kernel, outs, ins, out_specs, args, scratch=(), aliases=None, flops=0, moved=0, trans=0):
    return pl.pallas_call(
        kernel,
        out_shape=outs,
        in_specs=ins,
        out_specs=out_specs,
        scratch_shapes=list(scratch),
        input_output_aliases=aliases or {},
        compiler_params=pltpu.CompilerParams(vmem_limit_bytes=LIMIT),
        cost_estimate=pl.CostEstimate(flops=flops, bytes_accessed=moved, transcendentals=trans),
    )(*args)


def shape(dims, dtype=F32):
    return jax.ShapeDtypeStruct(dims, dtype)


def pack_kernel(par, gas, on, off, near, far, sems):
    ca, cr = gas.shape[1], gas.shape[2]
    odd_a, odd_r = par[0], par[1]
    copies = [
        pltpu.make_async_copy(gas.at[:, (ca - 1) * (1 - odd_a)], on, sems.at[0]),
        pltpu.make_async_copy(gas.at[:, (ca - 1) * odd_a], off, sems.at[1]),
        pltpu.make_async_copy(gas.at[:, :, (cr - 1) * (1 - odd_r)], near, sems.at[2]),
        pltpu.make_async_copy(gas.at[:, :, (cr - 1) * odd_r], far, sems.at[3]),
    ]
    for copy in copies:
        copy.start()
    for copy in copies:
        copy.wait()


def inner_terms(gas, transport, chemistry, tanh, a):
    nf, ca, cr, cz = gas.shape
    lane = iota((cr, cz), 1)
    row = iota((cr, cz), 0)
    for f in range(nf):
        nu, swirl, axial = transport[0, f], transport[1, f], transport[2, f]
        here = gas[f, a]
        total = -6.0 * nu * here
        total += (nu - 0.5 * axial) * jnp.where(lane == cz - 1, 0.0, pltpu.roll(here, cz - 1, 1))
        total += (nu + 0.5 * axial) * jnp.where(lane == 0, 0.0, pltpu.roll(here, 1, 1))
        radial = jnp.where(row == cr - 1, 0.0, pltpu.roll(here, cr - 1, 0))
        radial += jnp.where(row == 0, 0.0, pltpu.roll(here, 1, 0))
        total += nu * radial
        if a < ca - 1:
            total += (nu - 0.5 * swirl) * gas[f, a + 1]
        if a > 0:
            total += (nu + 0.5 * swirl) * gas[f, a - 1]
        for g in range(nf):
            total += chemistry[f, g] * tanh[g, a]
        yield f, total


def probe_all(gas, host, table, hots, probed):
    nf, ca, cr, cz = gas.shape
    slots = host.shape[1]
    width = ca * cz
    for f in range(nf):
        for a in range(ca):
            upper, lower = parts_of(gas[f, a], 2)
            table[f * cr : (f + 1) * cr, a * cz : (a + 1) * cz] = upper
            table[f * cr : (f + 1) * cr, width + a * cz : width + (a + 1) * cz] = lower
    span = cr * cz
    block = 256
    for b in range(slots // block):
        cells = host[:, b * block : (b + 1) * block]
        column = (cells // span) * cz + cells % cz
        row = (cells // cz) % cr
        hots[:, b * block : (b + 1) * block] = hot(iota((width, block), 0) == column)
        ahot = hots[:, b * block : (b + 1) * block]
        found = jnp.dot(table[:, :width], ahot, preferred_element_type=F32)
        found += jnp.dot(table[:, width:], ahot, preferred_element_type=F32)
        mask = iota((cr, block), 0) == row
        found = jnp.where(mask[None], found.reshape(nf, cr, block), 0.0)
        probed[:nf, b * block : (b + 1) * block] = jnp.sum(found, axis=1)


def react(probed, attr, live, evap, source_map):
    nf = source_map.shape[0]
    pull = evap[0] * probed[0:1]
    for f in range(1, nf):
        pull += evap[f] * probed[f : f + 1]
    sig = jax.nn.sigmoid(pull + attr[1:2])
    mdot = EVAP * attr[0:1] * sig * live
    source = source_map[:, 0:1] * attr[0:1]
    for k in range(1, source_map.shape[1]):
        source += source_map[:, k : k + 1] * attr[k : k + 1]
    source = source * mdot
    rows = [attr[0:1] - DT * mdot]
    rows.append(attr[1:2] + DT * RELAX * (probed[4:5] - attr[1:2]))
    rows.append(attr[2:5] + DT * RELAX * (probed[1:4] - attr[2:5]))
    rows.append(attr[5:8])
    return rows, source


def deposit_all(source, host, hots, shapes, reach, total):
    nf, ca, cr, cz = shapes
    width = ca * cz
    block = 512 if reach % 512 == 0 else 128
    for b in range(reach // block):
        cells = host[:, b * block : (b + 1) * block]
        row = (cells // cz) % cr
        mask = iota((cr, block), 0) == row
        spread = jnp.where(mask[None], source[:nf, b * block : (b + 1) * block][:, None, :], 0.0)
        upper, lower = parts_of(spread.reshape(nf * cr, block), 2)
        ahot = hots[:, b * block : (b + 1) * block]
        part = across(upper, ahot) + across(lower, ahot)
        if b == 0:
            total[...] = part
        else:
            total[...] += part


def list_hots(lists, section, slots, lhot):
    width = lists.shape[-1]
    for d in range(2):
        names = lists[0, 0, section, d : d + 1, :].astype(F32)
        column = jnp.broadcast_to(names, (width, width)).T
        for b in range(slots // width):
            at = iota((width, width), 1).astype(F32) + float(b * width)
            lhot[d * width : (d + 1) * width, b * width : (b + 1) * width] = hot(column == at)


def leave(parcels, lists, section, lhot, odd_a, span, slots):
    width = lists.shape[-1]
    parts = jnp.concatenate(parts_of(parcels[:, :slots], 3), axis=0)
    taken = across(parts, lhot[...])
    taken = taken[:ROWS] + taken[ROWS : 2 * ROWS] + taken[2 * ROWS :]
    gone = jnp.dot(jnp.ones((8, 2 * width), BF16), lhot[...], preferred_element_type=F32)
    live = jnp.where(gone[0:1] > 0.5, 0.0, parcels[LIVE : LIVE + 1, :slots])
    packs = []
    for d in range(2):
        valid = lists[0, 0, section, d : d + 1, :] < slots
        pack = taken[:, d * width : (d + 1) * width]
        cell = pack[HOST : HOST + 1].astype(jnp.int32) % span
        cell = jnp.where(valid, cell.astype(F32), -1.0)
        row = iota(pack.shape, 0)
        pack = jnp.where(row == HOST, cell, jnp.where(valid & (row < HOST), pack, 0.0))
        packs.append(pack)
    left, right = packs
    return jnp.where(odd_a == 1, left, right), jnp.where(odd_a == 1, right, left), live


def section_kernel(
    first, par, count, gas, transport, chemistry, evap, source_map, lists, *refs
):
    if first:
        mass, state, host_in, out, parcels, on, off = refs[:7]
        table, hots, probed, total, tanh, lhot = refs[7:]
    else:
        old_gas, old, out, parcels = refs[:4]
        table, hots, probed, total, tanh = refs[4:]
    nf, ca, cr, cz = gas.shape
    slots = probed.shape[1]
    reach = slots - 4 * lists.shape[-1]
    if first:
        host = host_in[0]
        live = (iota((1, slots), 1) < count[0, 0]).astype(F32)
        attr = jnp.concatenate([mass[0]] + [state[k, 0] for k in range(state.shape[0])], axis=0)
    else:
        host = old[HOST : HOST + 1, :slots].astype(jnp.int32)
        live = old[LIVE : LIVE + 1, :slots]
        attr = old[0:HOST, :slots]
    probe_all(gas, host, table, hots, probed)
    rows, source = react(probed[...], attr, live, evap, source_map)
    parcels[...] = jnp.zeros_like(parcels)
    parcels[0:ROWS, :slots] = jnp.concatenate(
        rows + [host.astype(F32), live, jnp.zeros((ROWS - LIVE - 1, slots), F32)], axis=0
    )
    if first:
        list_hots(lists, 0, slots, lhot)
        going_on, going_off, live_left = leave(parcels, lists, 0, lhot, par[0], cr * cz, slots)
        parcels[LIVE : LIVE + 1, :slots] = live_left
        on[...] = going_on
        off[...] = going_off
    for g in range(nf):
        tanh[g] = jnp.tanh(gas[g])
    deposit_all(source, host, hots, gas.shape, reach, total)
    for a in range(ca):
        for f, terms in inner_terms(gas, transport, chemistry, tanh, a):
            terms += total[f * cr : (f + 1) * cr, a * cz : (a + 1) * cz]
            here = gas[f, a] + DT * terms
            if not first:
                here = 0.5 * (old_gas[f, a] + here)
            out[f, a] = here


def edge_terms(scale, par, transport, out, on, off, near, far):
    nf, ca, cr, cz = out.shape
    odd_a, odd_r = par[0] == 1, par[1] == 1
    for f in range(nf):
        nu, swirl = transport[0, f], transport[1, f]
        got_on, got_off = on[f * cr : (f + 1) * cr], off[f * cr : (f + 1) * cr]
        east = jnp.where(odd_a, got_off, got_on)
        west = jnp.where(odd_a, got_on, got_off)
        out[f, 0] += (scale * (nu + 0.5 * swirl)) * west
        out[f, ca - 1] += (scale * (nu - 0.5 * swirl)) * east
        north = jnp.where(odd_r, far[f], near[f])
        south = jnp.where(odd_r, near[f], far[f])
        out[f, :, 0, :] += (scale * nu) * south
        out[f, :, cr - 1, :] += (scale * nu) * north


def edge_kernel(par, transport, base, on, off, near, far, pack_on, pack_off, out, *sends):
    send_on, send_off, send_near, send_far = sends
    nf, ca, cr, cz = out.shape
    out[...] = base[...]
    edge_terms(DT, par, transport, out, on, off, near, far)
    odd_a, odd_r = par[0] == 1, par[1] == 1
    for f in range(nf):
        low, high = out[f, 0], out[f, ca - 1]
        send_on[f * cr : (f + 1) * cr] = jnp.where(odd_a, low, high)
        send_off[f * cr : (f + 1) * cr] = jnp.where(odd_a, high, low)
        low, high = out[f, :, 0, :], out[f, :, cr - 1, :]
        send_near[f] = jnp.where(odd_r, low, high)
        send_far[f] = jnp.where(odd_r, high, low)
    send_on[nf * cr :] = pack_on[...]
    send_off[nf * cr :] = pack_off[...]


def put(parcels, pack, start, live):
    width = pack.shape[1]
    row = iota(pack.shape, 0)
    pack = jnp.where(row == LIVE, live, pack)
    shift = start % width
    first = pl.multiple_of((start // width) * width, width)
    pack = pltpu.roll(pack, shift, 1)
    lane = iota(pack.shape, 1)
    taken = pack[LIVE : LIVE + 1] > 0.5
    here = parcels[:, pl.ds(first, width)]
    parcels[:, pl.ds(first, width)] = jnp.where(taken & (lane >= shift), pack, here)
    second = pl.multiple_of(first + width, width)
    here = parcels[:, pl.ds(second, width)]
    parcels[:, pl.ds(second, width)] = jnp.where(taken & (lane < shift), pack, here)


def arrive_kernel(
    par, count, gas, evap, source_map, lists, on, off, old, parcels, send_on, send_off, sources,
    used, table, lhot,
):
    nf, ca, cr, cz = gas.shape
    slots = lhot.shape[1]
    odd_a = par[0] == 1
    base = nf * cr
    got_on, got_off = on[base:], off[base:]
    packs = [jnp.where(odd_a, got_on, got_off), jnp.where(odd_a, got_off, got_on)]
    parcels[...] = old[...]
    start = count[0, 0]
    for side in range(2):
        layer = side * (ca - 1)
        pack = packs[side]
        cell = pack[HOST : HOST + 1].astype(jnp.int32)
        live = (cell >= 0).astype(F32)
        for f in range(nf):
            upper, lower = parts_of(gas[f, layer], 2)
            table[f * cr : (f + 1) * cr, :cz] = upper
            table[f * cr : (f + 1) * cr, cz:] = lower
        zhot = hot(iota((cz, cell.shape[1]), 0) == cell % cz)
        found = jnp.dot(table[:, :cz], zhot, preferred_element_type=F32)
        found += jnp.dot(table[:, cz:], zhot, preferred_element_type=F32)
        mask = iota((cr, cell.shape[1]), 0) == cell // cz
        found = jnp.where(mask[None], found.reshape(nf, cr, cell.shape[1]), 0.0)
        probed = jnp.sum(found, axis=1)
        rows, source = react(probed, pack[0:HOST], live, evap, source_map)
        sources[side, :nf] = source
        sources[side, nf : nf + 1] = pack[HOST : HOST + 1]
        home = (cell + layer * cr * cz).astype(F32)
        moved = jnp.concatenate(rows + [home, live, jnp.zeros((ROWS - LIVE - 1, cell.shape[1]), F32)], 0)
        put(parcels, moved, start, live)
        start = start + jnp.sum(live).astype(jnp.int32)
    used[0, 0] = start
    list_hots(lists, 1, slots, lhot)
    going_on, going_off, live = leave(parcels, lists, 1, lhot, par[0], cr * cz, slots)
    parcels[LIVE : LIVE + 1, :slots] = live
    send_on[...] = going_on
    send_off[...] = going_off


def finish_kernel(par, transport, base, on, off, near, far, sources, out):
    nf, ca, cr, cz = out.shape
    out[...] = base[...]
    edge_terms(0.5 * DT, par, transport, out, on, off, near, far)
    for side in range(2):
        layer = side * (ca - 1)
        cell = sources[side, nf : nf + 1].astype(jnp.int32)
        mask = iota((cr, cell.shape[1]), 0) == cell // cz
        spread = jnp.where(mask[None], sources[side, :nf][:, None, :], 0.0)
        upper, lower = parts_of(spread.reshape(nf * cr, cell.shape[1]), 2)
        zhot = hot(iota((cz, cell.shape[1]), 0) == cell % cz)
        total = across(upper, zhot) + across(lower, zhot)
        for f in range(nf):
            out[f, layer] += (0.5 * DT) * total[f * cr : (f + 1) * cr]


def place_kernel(far_offset, par, count, on, off, old, mass, state, host, used, parcels):
    odd_a = par[0] == 1
    slots = mass.shape[-1]
    parcels[...] = old[...]
    got_on, got_off = on[...], off[...]
    packs = [jnp.where(odd_a, got_on, got_off), jnp.where(odd_a, got_off, got_on)]
    start = count[0, 0]
    for side in range(2):
        pack = packs[side]
        live = (pack[HOST : HOST + 1] >= 0.0).astype(F32)
        row = iota(pack.shape, 0)
        pack = jnp.where(row == HOST, pack + float(side * far_offset), pack)
        put(parcels, pack, start, live)
        start = start + jnp.sum(live).astype(jnp.int32)
    used[0, 0] = start
    live = parcels[LIVE : LIVE + 1, :slots] > 0.5
    mass[0] = jnp.where(live, parcels[0:1, :slots], 0.0)
    for k in range(state.shape[0]):
        state[k, 0] = jnp.where(live, parcels[k + 1 : k + 2, :slots], 0.0)
    host[0] = jnp.where(live, parcels[HOST : HOST + 1, :slots].astype(jnp.int32), -1)


def swap(array, axis, phase, wrap):
    size = lax.axis_size(axis)
    pairs = []
    for i in range(phase, size if wrap else size - 1, 2):
        j = (i + 1) % size
        pairs += [(i, j), (j, i)]
    return lax.ppermute(array, axis, pairs)


def on_device(
    gas, transport, chemistry, evap, source_map, mass, state, host, count, crossing
):
    nf, ca, cr, cz = gas.shape
    slots = mass.shape[-1]
    width = crossing.shape[-1]
    padded = slots + 2 * width
    par = jnp.stack([lax.axis_index("azim") % 2, lax.axis_index("radax") % 2]).astype(jnp.int32)
    layer, ring = shape((nf * cr, cz)), shape((nf, ca, cz))
    pack = shape((ROWS, width))
    on, off, near, far = call(
        pack_kernel,
        [shape((nf, cr, cz)), shape((nf, cr, cz)), ring, ring],
        [SMEM, ANY],
        [ANY] * 4,
        (par, gas),
        scratch=[pltpu.SemaphoreType.DMA((4,))],
        moved=2_000_000,
    )
    on = swap(on.reshape(nf * cr, cz), "azim", 0, True)
    off = swap(off.reshape(nf * cr, cz), "azim", 1, True)
    near = swap(near, "radax", 0, False)
    far = swap(far, "radax", 1, False)

    section_scratch = [
        pltpu.VMEM((nf * cr, 2 * ca * cz), BF16),
        pltpu.VMEM((ca * cz, slots), BF16),
        pltpu.VMEM((ROWS, slots), F32),
        pltpu.VMEM((nf * cr, ca * cz), F32),
        pltpu.VMEM(gas.shape, F32),
    ]
    list_scratch = pltpu.VMEM((2 * width, slots), BF16)
    heavy = dict(flops=6_000_000_000, moved=4_000_000, trans=300_000)
    params = [SMEM, SMEM, VMEM, SMEM, SMEM, SMEM, VMEM, VMEM]
    base, parcels, pack_on, pack_off = call(
        functools.partial(section_kernel, True),
        [shape(gas.shape), shape((ROWS, padded)), pack, pack],
        params + [VMEM] * 3,
        [VMEM] * 4,
        (par, count, gas, transport, chemistry, evap, source_map, crossing, mass, state, host),
        scratch=section_scratch + [list_scratch],
        **heavy,
    )
    longer = shape((nf * cr + ROWS, cz))
    section_one, on, off, near, far = call(
        edge_kernel,
        [shape(gas.shape), longer, longer, ring, ring],
        [SMEM, SMEM] + [VMEM] * 7,
        [VMEM] * 5,
        (par, transport, base, on, off, near, far, pack_on, pack_off),
        aliases={2: 0},
        moved=3_000_000,
    )
    on = swap(on, "azim", 0, True)
    off = swap(off, "azim", 1, True)
    near = swap(near, "radax", 0, False)
    far = swap(far, "radax", 1, False)
    base, parcels = call(
        functools.partial(section_kernel, False),
        [shape(gas.shape), shape((ROWS, padded))],
        params + [VMEM] * 2,
        [VMEM] * 2,
        (par, count, section_one, transport, chemistry, evap, source_map, crossing, gas, parcels),
        scratch=section_scratch,
        **heavy,
    )
    parcels, pack_on, pack_off, sources, count = call(
        arrive_kernel,
        [shape((ROWS, padded)), pack, pack, shape((2, ROWS, width)), shape((1, 1), jnp.int32)],
        [SMEM, SMEM, VMEM, SMEM] + [VMEM] * 5,
        [VMEM] * 4 + [SMEM],
        (par, count, section_one, evap, source_map, crossing, on, off, parcels),
        scratch=[pltpu.VMEM((nf * cr, 2 * cz), BF16), list_scratch],
        flops=100_000_000,
        moved=2_000_000,
    )
    pack_on = swap(pack_on, "azim", 0, True)
    pack_off = swap(pack_off, "azim", 1, True)
    gas_next = call(
        finish_kernel,
        shape(gas.shape),
        [SMEM, SMEM] + [VMEM] * 6,
        VMEM,
        (par, transport, base, on, off, near, far, sources),
        flops=100_000_000,
        moved=3_000_000,
    )
    mass_next, state_next, host_next, count_next = call(
        functools.partial(place_kernel, (ca - 1) * cr * cz),
        [shape(mass.shape), shape(state.shape), shape(host.shape, jnp.int32), shape((1, 1), jnp.int32)],
        [SMEM, SMEM] + [VMEM] * 3,
        [VMEM] * 3 + [SMEM],
        (par, count, pack_on, pack_off, parcels),
        scratch=[pltpu.VMEM((ROWS, padded), F32)],
        moved=500_000,
    )
    return gas_next, mass_next, state_next, host_next, count_next


def solution(mesh):
    in_specs = (
        P(None, "azim", "radax", None),
        P(),
        P(),
        P(),
        P(),
        P("azim", "radax", None),
        P(None, "azim", "radax", None),
        P("azim", "radax", None),
        P("azim", "radax"),
        P("azim", "radax", None, None, None),
    )
    out_specs = (
        P(None, "azim", "radax", None),
        P("azim", "radax", None),
        P(None, "azim", "radax", None),
        P("azim", "radax", None),
        P("azim", "radax"),
    )
    return jax.shard_map(
        on_device, mesh=mesh, in_specs=in_specs, out_specs=out_specs, check_vma=False
    )
```

```python
import functools

import jax
import jax.numpy as jnp
from jax import lax
from jax.experimental import pallas as pl
from jax.experimental.pallas import tpu as pltpu
from jax.sharding import PartitionSpec as P

DT = 0.5
RELAX = 0.3
EVAP = 0.5
F32 = jnp.float32
BF16 = jnp.bfloat16
ROWS = 16
HOST = 8
LIVE = 9
GONE = 10
LANES = 128
LIMIT = 40 << 20

VMEM = pl.BlockSpec(memory_space=pltpu.VMEM)
HBM = pl.BlockSpec(memory_space=pltpu.HBM)


def iota(shape, dim, dtype=jnp.int32):
    return lax.broadcasted_iota(dtype, shape, dim)


def parts_of(values, count):
    parts = []
    for _ in range(count - 1):
        part = values.astype(BF16)
        parts.append(part)
        values = values - part.astype(F32)
    return parts + [values.astype(BF16)]


def hot(mask):
    return mask.astype(F32).astype(BF16)


def across(left, right):
    return lax.dot_general(left, right, (((1,), (1,)), ((), ())), preferred_element_type=F32)


def call(kernel, outs, ins, out_specs, args, scratch=(), aliases=None, flops=0, moved=0, trans=0):
    return pl.pallas_call(
        kernel,
        out_shape=outs,
        in_specs=ins,
        out_specs=out_specs,
        scratch_shapes=list(scratch),
        input_output_aliases=aliases or {},
        compiler_params=pltpu.CompilerParams(vmem_limit_bytes=LIMIT),
        cost_estimate=pl.CostEstimate(flops=flops, bytes_accessed=moved, transcendentals=trans),
    )(*args)


def shape(dims, dtype=F32):
    return jax.ShapeDtypeStruct(dims, dtype)


def odd(axis):
    return lax.axis_index(axis) % 2


def pack_kernel(gas, *refs):
    small = (len(refs) - 3) // 2
    sources, (on, off), targets = refs[:small], refs[small : small + 2], refs[small + 2 : -1]
    sems = refs[-1]
    last = gas.shape[1] - 1
    flip = odd("azim")
    pairs = [(gas.at[:, last * flip], off), (gas.at[:, last * (1 - flip)], on)]
    pairs += list(zip(sources, targets))
    copies = [pltpu.make_async_copy(src, dst, sems.at[k]) for k, (src, dst) in enumerate(pairs)]
    for copy in copies:
        copy.start()
    for copy in copies:
        copy.wait()


def column_of(row):
    n = row.shape[1]
    square = jnp.broadcast_to(row, (n, n))
    return jnp.sum(jnp.where(iota((n, n), 0) == iota((n, n), 1), square, 0.0), axis=1, keepdims=True)


NU, UPPER, LOWER, EAST, WEST, PULL, SOURCE = range(7)


def fill_table(table, transport, chemistry, evap, source_map):
    nf = chemistry.shape[0]
    nu, swirl, axial = (column_of(transport[k : k + 1]) for k in range(3))
    columns = [nu, nu - 0.5 * axial, nu + 0.5 * axial, nu - 0.5 * swirl, nu + 0.5 * swirl]
    columns.append(column_of(evap[...]))
    columns += [column_of(source_map[k : k + 1]) for k in range(source_map.shape[0])]
    columns += [chemistry[:, g : g + 1] for g in range(nf)]
    for k, column in enumerate(columns):
        table[k, :nf] = jnp.broadcast_to(column, (nf, LANES))


def spread(table, k, f, rows):
    return jnp.broadcast_to(table[k, f : f + 1], (rows, LANES))


def inner_terms(gas, table, tanh):
    nf, ca, cr, cz = gas.shape
    lane = iota((cr, cz), 1)
    row = iota((cr, cz), 0)
    chem = table.shape[0] - nf
    for f in range(nf):
        nu, upper, lower, east, west = (spread(table, k, f, cr) for k in (NU, UPPER, LOWER, EAST, WEST))
        totals = []
        for a in range(ca):
            here = gas[f, a]
            total = nu * (
                jnp.where(row == cr - 1, 0.0, pltpu.roll(here, cr - 1, 0))
                + jnp.where(row == 0, 0.0, pltpu.roll(here, 1, 0))
                - 6.0 * here
            )
            total += upper * jnp.where(lane == cz - 1, 0.0, pltpu.roll(here, cz - 1, 1))
            total += lower * jnp.where(lane == 0, 0.0, pltpu.roll(here, 1, 1))
            if a < ca - 1:
                total += east * gas[f, a + 1]
            if a > 0:
                total += west * gas[f, a - 1]
            totals.append(total)
        for g in range(nf):
            rate = spread(table, chem + g, f, cr)
            for a in range(ca):
                totals[a] += rate * tanh[g, a]
        for a in range(ca):
            yield f, a, totals[a]


def probe_all(gas, host, table, hots, probed):
    nf, ca, cr, cz = gas.shape
    slots = host.shape[1]
    width = ca * cz
    for f in range(nf):
        for a in range(ca):
            upper, lower = parts_of(gas[f, a], 2)
            table[f * cr : (f + 1) * cr, a * cz : (a + 1) * cz] = upper
            table[f * cr : (f + 1) * cr, width + a * cz : width + (a + 1) * cz] = lower
    span = cr * cz
    block = 256
    for b in range(slots // block):
        cells = host[:, b * block : (b + 1) * block]
        column = (cells // span) * cz + cells % cz
        row = (cells // cz) % cr
        hots[:, b * block : (b + 1) * block] = hot(iota((width, block), 0) == column)
        ahot = hots[:, b * block : (b + 1) * block]
        found = jnp.dot(table[:, :width], ahot, preferred_element_type=F32)
        found += jnp.dot(table[:, width:], ahot, preferred_element_type=F32)
        mask = iota((cr, block), 0) == row
        found = jnp.where(mask[None], found.reshape(nf, cr, block), 0.0)
        probed[:nf, b * block : (b + 1) * block] = jnp.sum(found, axis=1)


def react(probed, attr, live, table, nf):
    pull = jnp.sum(table[PULL, :nf, 0:1] * probed[:nf], axis=0, keepdims=True)
    sig = jax.nn.sigmoid(pull + attr[1:2])
    mdot = EVAP * attr[0:1] * sig * live
    source = table[SOURCE, :nf, 0:1] * attr[0:1]
    for k in range(1, attr.shape[0]):
        source += table[SOURCE + k, :nf, 0:1] * attr[k : k + 1]
    source = source * mdot
    rows = [attr[0:1] - DT * mdot]
    rows.append(attr[1:2] + DT * RELAX * (probed[4:5] - attr[1:2]))
    rows.append(attr[2:5] + DT * RELAX * (probed[1:4] - attr[2:5]))
    rows.append(attr[5:8])
    return rows, source


def deposit_all(source, host, hots, shapes, reach, total):
    nf, ca, cr, cz = shapes
    width = ca * cz
    block = 512 if reach % 512 == 0 else 128
    for b in range(reach // block):
        cells = host[:, b * block : (b + 1) * block]
        row = (cells // cz) % cr
        mask = iota((cr, block), 0) == row
        spread = jnp.where(mask[None], source[:nf, b * block : (b + 1) * block][:, None, :], 0.0)
        upper, lower = parts_of(spread.reshape(nf * cr, block), 2)
        ahot = hots[:, b * block : (b + 1) * block]
        part = across(upper, ahot) + across(lower, ahot)
        if b == 0:
            total[...] = part
        else:
            total[...] += part


def list_hots(lists, section, slots, lhot):
    width = lists.shape[-1]
    for d in range(2):
        names = lists[0, 0, section, d : d + 1, :].astype(F32)
        column = jnp.broadcast_to(names, (width, width)).T
        for b in range(slots // width):
            at = iota((width, width), 1).astype(F32) + float(b * width)
            lhot[d * width : (d + 1) * width, b * width : (b + 1) * width] = hot(column == at)


def gather(parcels, lhot):
    parts = jnp.concatenate(parts_of(parcels, 3), axis=0)
    taken = across(parts, lhot)
    return taken[:ROWS] + taken[ROWS : 2 * ROWS] + taken[2 * ROWS :]


def gone_from(lhot):
    ones = jnp.ones((8, lhot.shape[0]), BF16)
    return jnp.dot(ones, lhot, preferred_element_type=F32)[0:1]


def packs_of(taken, lists, section, span, slots):
    width = lists.shape[-1]
    packs = []
    for d in range(2):
        valid = lists[0, 0, section, d : d + 1, :] < slots
        pack = taken[:, d * width : (d + 1) * width]
        cell = pack[HOST : HOST + 1].astype(jnp.int32) % span
        cell = jnp.where(valid, cell.astype(F32), -1.0)
        row = iota(pack.shape, 0)
        pack = jnp.where(row == HOST, cell, jnp.where(valid & (row < HOST), pack, 0.0))
        packs.append(pack)
    left, right = packs
    flip = odd("azim") == 1
    return jnp.where(flip, left, right), jnp.where(flip, right, left)


def send_rows(gas, near, far):
    cr = gas.shape[2]
    flip = odd("radax") == 1
    for f in range(gas.shape[0]):
        low, high = gas[f, :, 0, :], gas[f, :, cr - 1, :]
        near[f] = jnp.where(flip, low, high)
        far[f] = jnp.where(flip, high, low)


def probe_one_kernel(
    count, gas, transport, chemistry, evap, source_map, lists, mass, state, host_in,
    near, far, parcels, on, off, table, hots, source, cells, probed, lhot,
):
    nf, ca, cr, cz = gas.shape
    slots = probed.shape[1]
    send_rows(gas, near, far)
    fill_table(table, transport, chemistry, evap, source_map)
    host = host_in[0]
    live = (iota((1, slots), 1) < count[...]).astype(F32)
    attr = jnp.concatenate([mass[0]] + [state[k, 0] for k in range(state.shape[0])], axis=0)
    source[:nf] = parcel_work(gas, host, attr, live, table, parcels, cells, hots, probed)
    list_hots(lists, 0, slots, lhot)
    on[...], off[...] = packs_of(gather(parcels[:, :slots], lhot[...]), lists, 0, cr * cz, slots)
    parcels[LIVE : LIVE + 1, :slots] = jnp.where(gone_from(lhot[...]) > 0.5, 0.0, live)


def field_one_kernel(spare, gas, table, parcels, hots, source, out, total, tanh):
    nf, ca, cr, cz = gas.shape
    slots = hots.shape[1]
    for g in range(nf):
        tanh[g] = jnp.tanh(gas[g])
    host = parcels[HOST : HOST + 1, :slots].astype(jnp.int32)
    deposit_all(source, host, hots, gas.shape, slots - spare, total)
    for f, a, terms in inner_terms(gas, table, tanh):
        out[f, a] = gas[f, a] + DT * (terms + total[f * cr : (f + 1) * cr, a * cz : (a + 1) * cz])


def probe_two_kernel(
    gas, table, lists, old, near, far, parcels, hots, source, taken, lhot, cells, probed
):
    slots = probed.shape[1]
    send_rows(gas, near, far)
    host = old[HOST : HOST + 1, :slots].astype(jnp.int32)
    source[: gas.shape[0]] = parcel_work(
        gas, host, old[0:HOST, :slots], old[LIVE : LIVE + 1, :slots], table, parcels, cells, hots, probed
    )
    list_hots(lists, 1, slots, lhot)
    taken[...] = gather(parcels[:, :slots], lhot[...])
    parcels[GONE : GONE + 1, :slots] = gone_from(lhot[...])


def field_two_kernel(spare, gas, table, old_gas, parcels, hots, source, out, total, tanh):
    nf, ca, cr, cz = gas.shape
    slots = hots.shape[1]
    for g in range(nf):
        tanh[g] = jnp.tanh(gas[g])
    host = parcels[HOST : HOST + 1, :slots].astype(jnp.int32)
    deposit_all(source, host, hots, gas.shape, slots - spare, total)
    for f, a, terms in inner_terms(gas, table, tanh):
        terms += total[f * cr : (f + 1) * cr, a * cz : (a + 1) * cz]
        out[f, a] = 0.5 * (old_gas[f, a] + gas[f, a] + DT * terms)


def parcel_work(gas, host, attr, live, table, parcels, cells, hots, probed):
    slots = probed.shape[1]
    probe_all(gas, host, cells, hots, probed)
    rows, source = react(probed[...], attr, live, table, gas.shape[0])
    parcels[...] = jnp.zeros_like(parcels)
    parcels[0:ROWS, :slots] = jnp.concatenate(
        rows + [host.astype(F32), live, jnp.zeros((ROWS - LIVE - 1, slots), F32)], axis=0
    )
    return source


def edge_terms(scale, table, out, on, off, near, far):
    nf, ca, cr, cz = out.shape
    flip_a, flip_r = odd("azim") == 1, odd("radax") == 1
    for f in range(nf):
        got_on, got_off = on[f * cr : (f + 1) * cr], off[f * cr : (f + 1) * cr]
        east = jnp.where(flip_a, got_off, got_on)
        west = jnp.where(flip_a, got_on, got_off)
        out[f, 0] += (scale * spread(table, WEST, f, cr)) * west
        out[f, ca - 1] += (scale * spread(table, EAST, f, cr)) * east
        north = jnp.where(flip_r, far[f], near[f])
        south = jnp.where(flip_r, near[f], far[f])
        nu = scale * spread(table, NU, f, ca)
        out[f, :, 0, :] += nu * south
        out[f, :, cr - 1, :] += nu * north


def edge_kernel(table, base, on, off, near, far, pack_on, pack_off, out, send_on, send_off):
    nf, ca, cr, cz = out.shape
    out[...] = base[...]
    edge_terms(DT, table, out, on, off, near, far)
    flip = odd("azim") == 1
    for f in range(nf):
        low, high = out[f, 0], out[f, ca - 1]
        send_on[f * cr : (f + 1) * cr] = jnp.where(flip, low, high)
        send_off[f * cr : (f + 1) * cr] = jnp.where(flip, high, low)
    send_on[nf * cr :] = pack_on[...]
    send_off[nf * cr :] = pack_off[...]


def put(parcels, pack, start, live):
    width = pack.shape[1]
    row = iota(pack.shape, 0)
    pack = jnp.where(row == LIVE, live, pack)
    shift = start % width
    first = pl.multiple_of((start // width) * width, width)
    pack = pltpu.roll(pack, shift, 1)
    lane = iota(pack.shape, 1)
    taken = pack[LIVE : LIVE + 1] > 0.5
    here = parcels[:, pl.ds(first, width)]
    parcels[:, pl.ds(first, width)] = jnp.where(taken & (lane >= shift) & (row != GONE), pack, here)
    second = pl.multiple_of(first + width, width)
    here = parcels[:, pl.ds(second, width)]
    parcels[:, pl.ds(second, width)] = jnp.where(taken & (lane < shift) & (row != GONE), pack, here)


def sides(on, off):
    flip = odd("azim") == 1
    return jnp.where(flip, on, off), jnp.where(flip, off, on)


def scalar(ref):
    return jnp.sum(ref[...].astype(F32)).astype(jnp.int32)


def arrive_kernel(
    count, gas, table, lists, on, off, old, taken, lhot, parcels, send_on, send_off, sources, used, cells
):
    nf, ca, cr, cz = gas.shape
    slots = lhot.shape[1]
    base = nf * cr
    packs = sides(on[base:], off[base:])
    parcels[...] = old[...]
    start = scalar(count)
    for side in range(2):
        layer = side * (ca - 1)
        pack = packs[side]
        cell = pack[HOST : HOST + 1].astype(jnp.int32)
        live = (cell >= 0).astype(F32)
        for f in range(nf):
            upper, lower = parts_of(gas[f, layer], 2)
            cells[f * cr : (f + 1) * cr, :cz] = upper
            cells[f * cr : (f + 1) * cr, cz:] = lower
        zhot = hot(iota((cz, cell.shape[1]), 0) == cell % cz)
        found = jnp.dot(cells[:, :cz], zhot, preferred_element_type=F32)
        found += jnp.dot(cells[:, cz:], zhot, preferred_element_type=F32)
        mask = iota((cr, cell.shape[1]), 0) == cell // cz
        found = jnp.where(mask[None], found.reshape(nf, cr, cell.shape[1]), 0.0)
        probed = jnp.sum(found, axis=1)
        rows, source = react(probed, pack[0:HOST], live, table, nf)
        sources[side, :nf] = source
        sources[side, nf : nf + 1] = pack[HOST : HOST + 1]
        home = (cell + layer * cr * cz).astype(F32)
        moved = jnp.concatenate(rows + [home, live, jnp.zeros((ROWS - LIVE - 1, cell.shape[1]), F32)], 0)
        put(parcels, moved, start, live)
        start = start + jnp.sum(live).astype(jnp.int32)
    used[...] = jnp.broadcast_to(start, (1, 1))
    width = lists.shape[-1]
    first = pl.multiple_of(scalar(count), width)
    window = pl.ds(first, 2 * width)
    again = gather(parcels[:, window], lhot[:, window])
    names = jnp.concatenate([lists[0, 0, 1, d : d + 1, :] for d in range(2)], axis=1)
    inside = (names >= first) & (names < first + 2 * width)
    both = jnp.where(inside, again, taken[...])
    send_on[...], send_off[...] = packs_of(both, lists, 1, cr * cz, slots)
    gone = parcels[GONE : GONE + 1, :slots] > 0.5
    parcels[LIVE : LIVE + 1, :slots] = jnp.where(gone, 0.0, parcels[LIVE : LIVE + 1, :slots])


def finish_kernel(table, base, on, off, near, far, sources, out):
    nf, ca, cr, cz = out.shape
    out[...] = base[...]
    edge_terms(0.5 * DT, table, out, on, off, near, far)
    for side in range(2):
        layer = side * (ca - 1)
        cell = sources[side, nf : nf + 1].astype(jnp.int32)
        mask = iota((cr, cell.shape[1]), 0) == cell // cz
        laid = jnp.where(mask[None], sources[side, :nf][:, None, :], 0.0)
        upper, lower = parts_of(laid.reshape(nf * cr, cell.shape[1]), 2)
        zhot = hot(iota((cz, cell.shape[1]), 0) == cell % cz)
        total = across(upper, zhot) + across(lower, zhot)
        for f in range(nf):
            out[f, layer] += (0.5 * DT) * total[f * cr : (f + 1) * cr]


def place_kernel(far_offset, count, on, off, old, mass, state, host, used, parcels):
    slots = mass.shape[-1]
    parcels[...] = old[...]
    packs = sides(on[...], off[...])
    start = scalar(count)
    for side in range(2):
        pack = packs[side]
        live = (pack[HOST : HOST + 1] >= 0.0).astype(F32)
        row = iota(pack.shape, 0)
        pack = jnp.where(row == HOST, pack + float(side * far_offset), pack)
        put(parcels, pack, start, live)
        start = start + jnp.sum(live).astype(jnp.int32)
    used[...] = jnp.broadcast_to(start, (1, 1))
    live = parcels[LIVE : LIVE + 1, :slots] > 0.5
    mass[0] = jnp.where(live, parcels[0:1, :slots], 0.0)
    for k in range(state.shape[0]):
        state[k, 0] = jnp.where(live, parcels[k + 1 : k + 2, :slots], 0.0)
    host[0] = jnp.where(live, parcels[HOST : HOST + 1, :slots].astype(jnp.int32), -1)


def swap(array, axis, phase, wrap):
    size = lax.axis_size(axis)
    pairs = []
    for i in range(phase, size if wrap else size - 1, 2):
        j = (i + 1) % size
        pairs += [(i, j), (j, i)]
    return lax.ppermute(array, axis, pairs)


def on_device(
    gas, transport, chemistry, evap, source_map, mass, state, host, count, crossing
):
    nf, ca, cr, cz = gas.shape
    slots = mass.shape[-1]
    width = crossing.shape[-1]
    padded = slots + 2 * width
    ring, pack = shape((nf, ca, cz)), shape((ROWS, width))
    one = shape((1, 1), jnp.int32)
    grid, slotted = shape(gas.shape), shape((ROWS, padded))
    small = (gas, transport, chemistry, evap.reshape(1, nf), source_map.T, mass, state, host, crossing)
    on, off, *small = call(
        pack_kernel,
        [shape((nf, cr, cz)), shape((nf, cr, cz))] + [shape(v.shape, v.dtype) for v in small],
        [HBM] * (1 + len(small)),
        [VMEM] * (2 + len(small)),
        tuple(pltpu.with_memory_space_constraint(v, pltpu.HBM) for v in (gas,) + small),
        scratch=[pltpu.SemaphoreType.DMA((2 + len(small),))],
        moved=2_000_000,
    )
    gas, transport, chemistry, evap, source_map, mass, state, host, crossing = small
    off = swap(off.reshape(nf * cr, cz), "azim", 1, True)
    on = swap(on.reshape(nf * cr, cz), "azim", 0, True)

    hots, lhot = shape((ca * cz, slots), BF16), shape((2 * width, slots), BF16)
    source = shape((ROWS, slots))
    probe_scratch = [pltpu.VMEM((nf * cr, 2 * ca * cz), BF16), pltpu.VMEM((ROWS, slots), F32)]
    field_scratch = [pltpu.VMEM((nf * cr, ca * cz), F32), pltpu.VMEM(gas.shape, F32)]
    heavy = dict(flops=3_000_000_000, moved=2_000_000, trans=300_000)
    near, far, parcels, pack_on, pack_off, table, cell_hots, sources = call(
        probe_one_kernel,
        [ring, ring, slotted, pack, pack, shape((SOURCE + source_map.shape[0] + nf, ROWS, LANES)), hots, source],
        [VMEM] * 10,
        [VMEM] * 8,
        (count, gas, transport, chemistry, evap, source_map, crossing, mass, state, host),
        scratch=probe_scratch + [pltpu.VMEM(lhot.shape, BF16)],
        **heavy,
    )
    near = swap(near, "radax", 0, False)
    far = swap(far, "radax", 1, False)
    base = call(
        functools.partial(field_one_kernel, 4 * width),
        grid,
        [VMEM] * 5,
        VMEM,
        (gas, table, parcels, cell_hots, sources),
        scratch=field_scratch,
        flops=1_000_000,
        moved=10_000,
    )
    longer = shape((nf * cr + ROWS, cz))
    section_one, on, off = call(
        edge_kernel,
        [grid, longer, longer],
        [VMEM] * 8,
        [VMEM] * 3,
        (table, base, on, off, near, far, pack_on, pack_off),
        aliases={1: 0},
        moved=3_000_000,
    )
    off = swap(off, "azim", 1, True)
    on = swap(on, "azim", 0, True)
    near, far, parcels, cell_hots, sources, taken, named = call(
        probe_two_kernel,
        [ring, ring, slotted, hots, source, shape((ROWS, 2 * width)), lhot],
        [VMEM] * 4,
        [VMEM] * 7,
        (section_one, table, crossing, parcels),
        scratch=probe_scratch,
        **heavy,
    )
    near = swap(near, "radax", 0, False)
    far = swap(far, "radax", 1, False)
    base = call(
        functools.partial(field_two_kernel, 4 * width),
        grid,
        [VMEM] * 6,
        VMEM,
        (section_one, table, gas, parcels, cell_hots, sources),
        scratch=field_scratch,
        flops=1_000_000,
        moved=10_000,
    )
    parcels, pack_on, pack_off, sources, count = call(
        arrive_kernel,
        [slotted, pack, pack, shape((2, ROWS, width)), one],
        [VMEM] * 9,
        [VMEM] * 5,
        (count, section_one, table, crossing, on, off, parcels, taken, named),
        scratch=[pltpu.VMEM((nf * cr, 2 * cz), BF16)],
        flops=100_000_000,
        moved=2_000_000,
    )
    pack_off = swap(pack_off, "azim", 1, True)
    pack_on = swap(pack_on, "azim", 0, True)
    gas_next = call(
        finish_kernel,
        shape(gas.shape),
        [VMEM] * 7,
        VMEM,
        (table, base, on, off, near, far, sources),
        flops=100_000_000,
        moved=3_000_000,
    )
    mass_next, state_next, host_next, count_next = call(
        functools.partial(place_kernel, (ca - 1) * cr * cz),
        [shape(mass.shape), shape(state.shape), shape(host.shape, jnp.int32), one],
        [VMEM] * 4,
        [VMEM] * 4,
        (count, pack_on, pack_off, parcels),
        scratch=[pltpu.VMEM((ROWS, padded), F32)],
        moved=500_000,
    )
    return gas_next, mass_next, state_next, host_next, count_next


def solution(mesh):
    in_specs = (
        P(None, "azim", "radax", None),
        P(),
        P(),
        P(),
        P(),
        P("azim", "radax", None),
        P(None, "azim", "radax", None),
        P("azim", "radax", None),
        P("azim", "radax"),
        P("azim", "radax", None, None, None),
    )
    out_specs = (
        P(None, "azim", "radax", None),
        P("azim", "radax", None),
        P(None, "azim", "radax", None),
        P("azim", "radax", None),
        P("azim", "radax"),
    )
    return jax.shard_map(
        on_device, mesh=mesh, in_specs=in_specs, out_specs=out_specs, check_vma=False
    )
```

```python
import functools

import jax
import jax.numpy as jnp
from jax import lax
from jax.experimental import pallas as pl
from jax.experimental.pallas import tpu as pltpu
from jax.sharding import PartitionSpec as P

DT = 0.5
RELAX = 0.3
EVAP = 0.5
F32 = jnp.float32
BF16 = jnp.bfloat16
ROWS = 16
HOST = 8
LIVE = 9
GONE = 10
LANES = 128
LIMIT = 40 << 20

VMEM = pl.BlockSpec(memory_space=pltpu.VMEM)
HBM = pl.BlockSpec(memory_space=pltpu.HBM)


def iota(shape, dim, dtype=jnp.int32):
    return lax.broadcasted_iota(dtype, shape, dim)


def parts_of(values, count):
    parts = []
    for _ in range(count - 1):
        part = values.astype(BF16)
        parts.append(part)
        values = values - part.astype(F32)
    return parts + [values.astype(BF16)]


def hot(mask):
    return mask.astype(F32).astype(BF16)


def across(left, right):
    return lax.dot_general(left, right, (((1,), (1,)), ((), ())), preferred_element_type=F32)


def call(kernel, outs, ins, out_specs, args, scratch=(), aliases=None, flops=0, moved=0, trans=0):
    return pl.pallas_call(
        kernel,
        out_shape=outs,
        in_specs=ins,
        out_specs=out_specs,
        scratch_shapes=list(scratch),
        input_output_aliases=aliases or {},
        compiler_params=pltpu.CompilerParams(vmem_limit_bytes=LIMIT),
        cost_estimate=pl.CostEstimate(flops=flops, bytes_accessed=moved, transcendentals=trans),
    )(*args)


def shape(dims, dtype=F32):
    return jax.ShapeDtypeStruct(dims, dtype)


def odd(axis):
    return lax.axis_index(axis) % 2


def pack_kernel(gas, *refs):
    small = (len(refs) - 3) // 2
    sources, (on, off), targets = refs[:small], refs[small : small + 2], refs[small + 2 : -1]
    sems = refs[-1]
    last = gas.shape[1] - 1
    flip = odd("azim")
    pairs = [(gas.at[:, last * flip], off), (gas.at[:, last * (1 - flip)], on)]
    pairs += list(zip(sources, targets))
    copies = [pltpu.make_async_copy(src, dst, sems.at[k]) for k, (src, dst) in enumerate(pairs)]
    for copy in copies:
        copy.start()
    for copy in copies:
        copy.wait()


def column_of(row):
    n = row.shape[1]
    square = jnp.broadcast_to(row, (n, n))
    return jnp.sum(jnp.where(iota((n, n), 0) == iota((n, n), 1), square, 0.0), axis=1, keepdims=True)


NU, UPPER, LOWER, EAST, WEST, PULL, SOURCE = range(7)


def fill_table(table, transport, chemistry, evap, source_map):
    nf = chemistry.shape[0]
    nu, swirl, axial = (column_of(transport[k : k + 1]) for k in range(3))
    columns = [nu, nu - 0.5 * axial, nu + 0.5 * axial, nu - 0.5 * swirl, nu + 0.5 * swirl]
    columns.append(column_of(evap[...]))
    columns += [column_of(source_map[k : k + 1]) for k in range(source_map.shape[0])]
    columns += [chemistry[:, g : g + 1] for g in range(nf)]
    for k, column in enumerate(columns):
        table[k, :nf] = jnp.broadcast_to(column, (nf, LANES))


def spread(table, k, f, rows):
    return jnp.broadcast_to(table[k, f : f + 1], (rows, LANES))


def inner_terms(gas, table, tanh):
    nf, ca, cr, cz = gas.shape
    lane = iota((cr, cz), 1)
    row = iota((cr, cz), 0)
    chem = table.shape[0] - nf
    for f in range(nf):
        nu, upper, lower, east, west = (spread(table, k, f, cr) for k in (NU, UPPER, LOWER, EAST, WEST))
        totals = []
        for a in range(ca):
            here = gas[f, a]
            total = nu * (
                jnp.where(row == cr - 1, 0.0, pltpu.roll(here, cr - 1, 0))
                + jnp.where(row == 0, 0.0, pltpu.roll(here, 1, 0))
                - 6.0 * here
            )
            total += upper * jnp.where(lane == cz - 1, 0.0, pltpu.roll(here, cz - 1, 1))
            total += lower * jnp.where(lane == 0, 0.0, pltpu.roll(here, 1, 1))
            if a < ca - 1:
                total += east * gas[f, a + 1]
            if a > 0:
                total += west * gas[f, a - 1]
            totals.append(total)
        for g in range(nf):
            rate = spread(table, chem + g, f, cr)
            for a in range(ca):
                totals[a] += rate * tanh[g, a]
        for a in range(ca):
            yield f, a, totals[a]


def probe_all(gas, host, table, hots, probed):
    nf, ca, cr, cz = gas.shape
    slots = host.shape[1]
    width = ca * cz
    for f in range(nf):
        for a in range(ca):
            upper, lower = parts_of(gas[f, a], 2)
            table[f * cr : (f + 1) * cr, a * cz : (a + 1) * cz] = upper
            table[f * cr : (f + 1) * cr, width + a * cz : width + (a + 1) * cz] = lower
    span = cr * cz
    block = 256
    for b in range(slots // block):
        cells = host[:, b * block : (b + 1) * block]
        column = (cells // span) * cz + cells % cz
        row = (cells // cz) % cr
        hots[:, b * block : (b + 1) * block] = hot(iota((width, block), 0) == column)
        ahot = hots[:, b * block : (b + 1) * block]
        found = jnp.dot(table[:, :width], ahot, preferred_element_type=F32)
        found += jnp.dot(table[:, width:], ahot, preferred_element_type=F32)
        mask = iota((cr, block), 0) == row
        found = jnp.where(mask[None], found.reshape(nf, cr, block), 0.0)
        probed[:nf, b * block : (b + 1) * block] = jnp.sum(found, axis=1)


def react(probed, attr, live, table, nf):
    pull = jnp.sum(table[PULL, :nf, 0:1] * probed[:nf], axis=0, keepdims=True)
    sig = jax.nn.sigmoid(pull + attr[1:2])
    mdot = EVAP * attr[0:1] * sig * live
    source = table[SOURCE, :nf, 0:1] * attr[0:1]
    for k in range(1, attr.shape[0]):
        source += table[SOURCE + k, :nf, 0:1] * attr[k : k + 1]
    source = source * mdot
    rows = [attr[0:1] - DT * mdot]
    rows.append(attr[1:2] + DT * RELAX * (probed[4:5] - attr[1:2]))
    rows.append(attr[2:5] + DT * RELAX * (probed[1:4] - attr[2:5]))
    rows.append(attr[5:8])
    return rows, source


def deposit_all(source, host, hots, shapes, reach, total):
    nf, ca, cr, cz = shapes
    width = ca * cz
    block = 512 if reach % 512 == 0 else 128
    for b in range(reach // block):
        cells = host[:, b * block : (b + 1) * block]
        row = (cells // cz) % cr
        mask = iota((cr, block), 0) == row
        spread = jnp.where(mask[None], source[:nf, b * block : (b + 1) * block][:, None, :], 0.0)
        upper, lower = parts_of(spread.reshape(nf * cr, block), 2)
        ahot = hots[:, b * block : (b + 1) * block]
        part = across(upper, ahot) + across(lower, ahot)
        if b == 0:
            total[...] = part
        else:
            total[...] += part


def list_hots(lists, section, slots, lhot):
    width = lists.shape[-1]
    for d in range(2):
        names = lists[0, 0, section, d : d + 1, :].astype(F32)
        column = jnp.broadcast_to(names, (width, width)).T
        for b in range(slots // width):
            at = iota((width, width), 1).astype(F32) + float(b * width)
            lhot[d * width : (d + 1) * width, b * width : (b + 1) * width] = hot(column == at)


def gather(parcels, lhot):
    parts = jnp.concatenate(parts_of(parcels, 3), axis=0)
    taken = across(parts, lhot)
    return taken[:ROWS] + taken[ROWS : 2 * ROWS] + taken[2 * ROWS :]


def gone_from(lhot):
    ones = jnp.ones((8, lhot.shape[0]), BF16)
    return jnp.dot(ones, lhot, preferred_element_type=F32)[0:1]


def packs_of(taken, lists, section, span, slots):
    width = lists.shape[-1]
    packs = []
    for d in range(2):
        valid = lists[0, 0, section, d : d + 1, :] < slots
        pack = taken[:, d * width : (d + 1) * width]
        cell = pack[HOST : HOST + 1].astype(jnp.int32) % span
        cell = jnp.where(valid, cell.astype(F32), -1.0)
        row = iota(pack.shape, 0)
        pack = jnp.where(row == HOST, cell, jnp.where(valid & (row < HOST), pack, 0.0))
        packs.append(pack)
    left, right = packs
    flip = odd("azim") == 1
    return jnp.where(flip, left, right), jnp.where(flip, right, left)


def send_rows(gas, near, far):
    cr = gas.shape[2]
    flip = odd("radax") == 1
    for f in range(gas.shape[0]):
        low, high = gas[f, :, 0, :], gas[f, :, cr - 1, :]
        near[f] = jnp.where(flip, low, high)
        far[f] = jnp.where(flip, high, low)


def probe_one_kernel(
    count, gas, transport, chemistry, evap, source_map, lists, mass, state, host_in,
    near, far, parcels, on, off, table, hots, source, cells, probed, lhot,
):
    nf, ca, cr, cz = gas.shape
    slots = probed.shape[1]
    send_rows(gas, near, far)
    fill_table(table, transport, chemistry, evap, source_map)
    host = host_in[0]
    live = (iota((1, slots), 1) < count[...]).astype(F32)
    attr = jnp.concatenate([mass[0]] + [state[k, 0] for k in range(state.shape[0])], axis=0)
    source[:nf] = parcel_work(gas, host, attr, live, table, parcels, cells, hots, probed)
    list_hots(lists, 0, slots, lhot)
    on[...], off[...] = packs_of(gather(parcels[:, :slots], lhot[...]), lists, 0, cr * cz, slots)
    parcels[LIVE : LIVE + 1, :slots] = jnp.where(gone_from(lhot[...]) > 0.5, 0.0, live)


def field_one_kernel(spare, gas, table, parcels, hots, source, out, total, tanh):
    nf, ca, cr, cz = gas.shape
    slots = hots.shape[1]
    for g in range(nf):
        tanh[g] = jnp.tanh(gas[g])
    host = parcels[HOST : HOST + 1, :slots].astype(jnp.int32)
    deposit_all(source, host, hots, gas.shape, slots - spare, total)
    for f, a, terms in inner_terms(gas, table, tanh):
        out[f, a] = gas[f, a] + DT * (terms + total[f * cr : (f + 1) * cr, a * cz : (a + 1) * cz])


def probe_two_kernel(
    gas, table, lists, old, near, far, parcels, hots, source, taken, lhot, cells, probed
):
    slots = probed.shape[1]
    send_rows(gas, near, far)
    host = old[HOST : HOST + 1, :slots].astype(jnp.int32)
    source[: gas.shape[0]] = parcel_work(
        gas, host, old[0:HOST, :slots], old[LIVE : LIVE + 1, :slots], table, parcels, cells, hots, probed
    )
    list_hots(lists, 1, slots, lhot)
    taken[...] = gather(parcels[:, :slots], lhot[...])
    parcels[GONE : GONE + 1, :slots] = gone_from(lhot[...])


def field_two_kernel(spare, gas, table, old_gas, parcels, hots, source, out, total, tanh):
    nf, ca, cr, cz = gas.shape
    slots = hots.shape[1]
    for g in range(nf):
        tanh[g] = jnp.tanh(gas[g])
    host = parcels[HOST : HOST + 1, :slots].astype(jnp.int32)
    deposit_all(source, host, hots, gas.shape, slots - spare, total)
    for f, a, terms in inner_terms(gas, table, tanh):
        terms += total[f * cr : (f + 1) * cr, a * cz : (a + 1) * cz]
        out[f, a] = 0.5 * (old_gas[f, a] + gas[f, a] + DT * terms)


def parcel_work(gas, host, attr, live, table, parcels, cells, hots, probed):
    slots = probed.shape[1]
    probe_all(gas, host, cells, hots, probed)
    rows, source = react(probed[...], attr, live, table, gas.shape[0])
    parcels[...] = jnp.zeros_like(parcels)
    parcels[0:ROWS, :slots] = jnp.concatenate(
        rows + [host.astype(F32), live, jnp.zeros((ROWS - LIVE - 1, slots), F32)], axis=0
    )
    return source


def edge_terms(scale, table, out, on, off, near, far):
    nf, ca, cr, cz = out.shape
    block = lax.axis_index("radax")
    inner, outer = block == 0, block == lax.axis_size("radax") - 1
    flip_a, flip_r = odd("azim") == 1, odd("radax") == 1
    for f in range(nf):
        got_on, got_off = on[f * cr : (f + 1) * cr], off[f * cr : (f + 1) * cr]
        east = jnp.where(flip_a, got_off, got_on)
        west = jnp.where(flip_a, got_on, got_off)
        out[f, 0] += (scale * spread(table, WEST, f, cr)) * west
        out[f, ca - 1] += (scale * spread(table, EAST, f, cr)) * east
        north = jnp.where(outer, 0.0, jnp.where(flip_r, far[f], near[f]))
        south = jnp.where(inner, 0.0, jnp.where(flip_r, near[f], far[f]))
        nu = scale * spread(table, NU, f, ca)
        out[f, :, 0, :] += nu * south
        out[f, :, cr - 1, :] += nu * north


def edge_kernel(table, base, off, on, far, near, pack_on, pack_off, out, send_on, send_off):
    nf, ca, cr, cz = out.shape
    out[...] = base[...]
    edge_terms(DT, table, out, on, off, near, far)
    flip = odd("azim") == 1
    for f in range(nf):
        low, high = out[f, 0], out[f, ca - 1]
        send_on[f * cr : (f + 1) * cr] = jnp.where(flip, low, high)
        send_off[f * cr : (f + 1) * cr] = jnp.where(flip, high, low)
    send_on[nf * cr :] = pack_on[...]
    send_off[nf * cr :] = pack_off[...]


def put(parcels, pack, start, live):
    width = pack.shape[1]
    row = iota(pack.shape, 0)
    pack = jnp.where(row == LIVE, live, pack)
    shift = start % width
    first = pl.multiple_of((start // width) * width, width)
    pack = pltpu.roll(pack, shift, 1)
    lane = iota(pack.shape, 1)
    taken = pack[LIVE : LIVE + 1] > 0.5
    here = parcels[:, pl.ds(first, width)]
    parcels[:, pl.ds(first, width)] = jnp.where(taken & (lane >= shift) & (row != GONE), pack, here)
    second = pl.multiple_of(first + width, width)
    here = parcels[:, pl.ds(second, width)]
    parcels[:, pl.ds(second, width)] = jnp.where(taken & (lane < shift) & (row != GONE), pack, here)


def sides(on, off):
    flip = odd("azim") == 1
    return jnp.where(flip, on, off), jnp.where(flip, off, on)


def scalar(ref):
    return jnp.sum(ref[...].astype(F32)).astype(jnp.int32)


def arrive_kernel(
    count, gas, table, lists, on, off, old, taken, lhot, parcels, send_on, send_off, sources, used, cells
):
    nf, ca, cr, cz = gas.shape
    slots = lhot.shape[1]
    base = nf * cr
    packs = sides(on[base:], off[base:])
    parcels[...] = old[...]
    start = scalar(count)
    for side in range(2):
        layer = side * (ca - 1)
        pack = packs[side]
        cell = pack[HOST : HOST + 1].astype(jnp.int32)
        live = (cell >= 0).astype(F32)
        for f in range(nf):
            upper, lower = parts_of(gas[f, layer], 2)
            cells[f * cr : (f + 1) * cr, :cz] = upper
            cells[f * cr : (f + 1) * cr, cz:] = lower
        zhot = hot(iota((cz, cell.shape[1]), 0) == cell % cz)
        found = jnp.dot(cells[:, :cz], zhot, preferred_element_type=F32)
        found += jnp.dot(cells[:, cz:], zhot, preferred_element_type=F32)
        mask = iota((cr, cell.shape[1]), 0) == cell // cz
        found = jnp.where(mask[None], found.reshape(nf, cr, cell.shape[1]), 0.0)
        probed = jnp.sum(found, axis=1)
        rows, source = react(probed, pack[0:HOST], live, table, nf)
        sources[side, :nf] = source
        sources[side, nf : nf + 1] = pack[HOST : HOST + 1]
        home = (cell + layer * cr * cz).astype(F32)
        moved = jnp.concatenate(rows + [home, live, jnp.zeros((ROWS - LIVE - 1, cell.shape[1]), F32)], 0)
        put(parcels, moved, start, live)
        start = start + jnp.sum(live).astype(jnp.int32)
    used[...] = jnp.broadcast_to(start, (1, 1))
    width = lists.shape[-1]
    first = pl.multiple_of(scalar(count), width)
    window = pl.ds(first, 2 * width)
    again = gather(parcels[:, window], lhot[:, window])
    names = jnp.concatenate([lists[0, 0, 1, d : d + 1, :] for d in range(2)], axis=1)
    inside = (names >= first) & (names < first + 2 * width)
    both = jnp.where(inside, again, taken[...])
    send_on[...], send_off[...] = packs_of(both, lists, 1, cr * cz, slots)
    gone = parcels[GONE : GONE + 1, :slots] > 0.5
    parcels[LIVE : LIVE + 1, :slots] = jnp.where(gone, 0.0, parcels[LIVE : LIVE + 1, :slots])


def finish_kernel(table, base, off, on, near, far, sources, out):
    nf, ca, cr, cz = out.shape
    out[...] = base[...]
    edge_terms(0.5 * DT, table, out, on, off, near, far)
    for side in range(2):
        layer = side * (ca - 1)
        cell = sources[side, nf : nf + 1].astype(jnp.int32)
        mask = iota((cr, cell.shape[1]), 0) == cell // cz
        laid = jnp.where(mask[None], sources[side, :nf][:, None, :], 0.0)
        upper, lower = parts_of(laid.reshape(nf * cr, cell.shape[1]), 2)
        zhot = hot(iota((cz, cell.shape[1]), 0) == cell % cz)
        total = across(upper, zhot) + across(lower, zhot)
        for f in range(nf):
            out[f, layer] += (0.5 * DT) * total[f * cr : (f + 1) * cr]


def place_kernel(far_offset, count, off, on, old, mass, state, host, used, parcels):
    slots = mass.shape[-1]
    parcels[...] = old[...]
    packs = sides(on[...], off[...])
    start = scalar(count)
    for side in range(2):
        pack = packs[side]
        live = (pack[HOST : HOST + 1] >= 0.0).astype(F32)
        row = iota(pack.shape, 0)
        pack = jnp.where(row == HOST, pack + float(side * far_offset), pack)
        put(parcels, pack, start, live)
        start = start + jnp.sum(live).astype(jnp.int32)
    used[...] = jnp.broadcast_to(start, (1, 1))
    live = parcels[LIVE : LIVE + 1, :slots] > 0.5
    mass[0] = jnp.where(live, parcels[0:1, :slots], 0.0)
    for k in range(state.shape[0]):
        state[k, 0] = jnp.where(live, parcels[k + 1 : k + 2, :slots], 0.0)
    host[0] = jnp.where(live, parcels[HOST : HOST + 1, :slots].astype(jnp.int32), -1)


def swap(array, axis, phase):
    size = lax.axis_size(axis)
    pairs = []
    for i in range(phase, size + phase, 2):
        j = (i + 1) % size
        pairs += [(i, j), (j, i)]
    return lax.ppermute(array, axis, pairs)


def swap_rows(array, phase):
    sectors, blocks = lax.axis_size("azim"), lax.axis_size("radax")
    pairs = []
    for i in range(sectors):
        for j in range(blocks):
            other = j + 1 if (j - phase) % 2 == 0 else j - 1
            target = (i, other) if 0 <= other < blocks else (i ^ 1, j)
            pairs.append((i * blocks + j, target[0] * blocks + target[1]))
    return lax.ppermute(array, ("azim", "radax"), pairs)


def on_device(
    gas, transport, chemistry, evap, source_map, mass, state, host, count, crossing
):
    nf, ca, cr, cz = gas.shape
    slots = mass.shape[-1]
    width = crossing.shape[-1]
    padded = slots + 2 * width
    ring, pack = shape((nf, ca, cz)), shape((ROWS, width))
    one = shape((1, 1), jnp.int32)
    grid, slotted = shape(gas.shape), shape((ROWS, padded))
    small = (gas, transport, chemistry, evap.reshape(1, nf), source_map.T, mass, state, host, crossing)
    on, off, *small = call(
        pack_kernel,
        [shape((nf, cr, cz)), shape((nf, cr, cz))] + [shape(v.shape, v.dtype) for v in small],
        [HBM] * (1 + len(small)),
        [VMEM] * (2 + len(small)),
        tuple(pltpu.with_memory_space_constraint(v, pltpu.HBM) for v in (gas,) + small),
        scratch=[pltpu.SemaphoreType.DMA((2 + len(small),))],
        moved=2_000_000,
    )
    gas, transport, chemistry, evap, source_map, mass, state, host, crossing = small
    off = swap(off.reshape(nf * cr, cz), "azim", 1)
    on = swap(on.reshape(nf * cr, cz), "azim", 0)

    hots, lhot = shape((ca * cz, slots), BF16), shape((2 * width, slots), BF16)
    source = shape((ROWS, slots))
    probe_scratch = [pltpu.VMEM((nf * cr, 2 * ca * cz), BF16), pltpu.VMEM((ROWS, slots), F32)]
    field_scratch = [pltpu.VMEM((nf * cr, ca * cz), F32), pltpu.VMEM(gas.shape, F32)]
    heavy = dict(flops=3_000_000_000, moved=2_000_000, trans=300_000)
    near, far, parcels, pack_on, pack_off, table, cell_hots, sources = call(
        probe_one_kernel,
        [ring, ring, slotted, pack, pack, shape((SOURCE + source_map.shape[0] + nf, ROWS, LANES)), hots, source],
        [VMEM] * 10,
        [VMEM] * 8,
        (count, gas, transport, chemistry, evap, source_map, crossing, mass, state, host),
        scratch=probe_scratch + [pltpu.VMEM(lhot.shape, BF16)],
        **heavy,
    )
    near = swap_rows(near, 0)
    far = swap_rows(far, 1)
    base = call(
        functools.partial(field_one_kernel, 4 * width),
        grid,
        [VMEM] * 5,
        VMEM,
        (gas, table, parcels, cell_hots, sources),
        scratch=field_scratch,
        flops=1_000_000,
        moved=10_000,
    )
    longer = shape((nf * cr + ROWS, cz))
    section_one, on, off = call(
        edge_kernel,
        [grid, longer, longer],
        [VMEM] * 8,
        [VMEM] * 3,
        (table, base, off, on, far, near, pack_on, pack_off),
        aliases={1: 0},
        moved=3_000_000,
    )
    off = swap(off, "azim", 1)
    on = swap(on, "azim", 0)
    near, far, parcels, cell_hots, sources, taken, named = call(
        probe_two_kernel,
        [ring, ring, slotted, hots, source, shape((ROWS, 2 * width)), lhot],
        [VMEM] * 4,
        [VMEM] * 7,
        (section_one, table, crossing, parcels),
        scratch=probe_scratch,
        **heavy,
    )
    near = swap_rows(near, 0)
    far = swap_rows(far, 1)
    base = call(
        functools.partial(field_two_kernel, 4 * width),
        grid,
        [VMEM] * 6,
        VMEM,
        (section_one, table, gas, parcels, cell_hots, sources),
        scratch=field_scratch,
        flops=1_000_000,
        moved=10_000,
    )
    parcels, pack_on, pack_off, sources, count = call(
        arrive_kernel,
        [slotted, pack, pack, shape((2, ROWS, width)), one],
        [VMEM] * 9,
        [VMEM] * 5,
        (count, section_one, table, crossing, on, off, parcels, taken, named),
        scratch=[pltpu.VMEM((nf * cr, 2 * cz), BF16)],
        flops=100_000_000,
        moved=2_000_000,
    )
    pack_off = swap(pack_off, "azim", 1)
    pack_on = swap(pack_on, "azim", 0)
    gas_next = call(
        finish_kernel,
        shape(gas.shape),
        [VMEM] * 7,
        VMEM,
        (table, base, off, on, near, far, sources),
        flops=100_000_000,
        moved=3_000_000,
    )
    mass_next, state_next, host_next, count_next = call(
        functools.partial(place_kernel, (ca - 1) * cr * cz),
        [shape(mass.shape), shape(state.shape), shape(host.shape, jnp.int32), one],
        [VMEM] * 4,
        [VMEM] * 4,
        (count, pack_off, pack_on, parcels),
        scratch=[pltpu.VMEM((ROWS, padded), F32)],
        moved=500_000,
    )
    return gas_next, mass_next, state_next, host_next, count_next


def solution(mesh):
    in_specs = (
        P(None, "azim", "radax", None),
        P(),
        P(),
        P(),
        P(),
        P("azim", "radax", None),
        P(None, "azim", "radax", None),
        P("azim", "radax", None),
        P("azim", "radax"),
        P("azim", "radax", None, None, None),
    )
    out_specs = (
        P(None, "azim", "radax", None),
        P("azim", "radax", None),
        P(None, "azim", "radax", None),
        P("azim", "radax", None),
        P("azim", "radax"),
    )
    return jax.shard_map(
        on_device, mesh=mesh, in_specs=in_specs, out_specs=out_specs, check_vma=False
    )
```

```python
import functools

import jax
import jax.numpy as jnp
from jax import lax
from jax.experimental import pallas as pl
from jax.experimental.pallas import tpu as pltpu
from jax.sharding import PartitionSpec as P

DT = 0.5
RELAX = 0.3
EVAP = 0.5
F32 = jnp.float32
BF16 = jnp.bfloat16
ROWS = 16
HOST = 8
LIVE = 9
GONE = 10
LANES = 128
LIMIT = 40 << 20

VMEM = pl.BlockSpec(memory_space=pltpu.VMEM)
HBM = pl.BlockSpec(memory_space=pltpu.HBM)


def iota(shape, dim, dtype=jnp.int32):
    return lax.broadcasted_iota(dtype, shape, dim)


def parts_of(values, count):
    parts = []
    for _ in range(count - 1):
        part = values.astype(BF16)
        parts.append(part)
        values = values - part.astype(F32)
    return parts + [values.astype(BF16)]


def hot(mask):
    return mask.astype(F32).astype(BF16)


def across(left, right):
    return lax.dot_general(left, right, (((1,), (1,)), ((), ())), preferred_element_type=F32)


def call(kernel, outs, ins, out_specs, args, scratch=(), aliases=None, flops=0, moved=0, trans=0):
    return pl.pallas_call(
        kernel,
        out_shape=outs,
        in_specs=ins,
        out_specs=out_specs,
        scratch_shapes=list(scratch),
        input_output_aliases=aliases or {},
        compiler_params=pltpu.CompilerParams(vmem_limit_bytes=LIMIT),
        cost_estimate=pl.CostEstimate(flops=flops, bytes_accessed=moved, transcendentals=trans),
    )(*args)


def shape(dims, dtype=F32):
    return jax.ShapeDtypeStruct(dims, dtype)


def odd(axis):
    return lax.axis_index(axis) % 2


def pack_kernel(gas, *refs):
    small = (len(refs) - 3) // 2
    sources, (on, off), targets = refs[:small], refs[small : small + 2], refs[small + 2 : -1]
    sems = refs[-1]
    last = gas.shape[1] - 1
    flip = odd("azim")
    pairs = [(gas.at[:, last * flip], off), (gas.at[:, last * (1 - flip)], on)]
    pairs += list(zip(sources, targets))
    copies = [pltpu.make_async_copy(src, dst, sems.at[k]) for k, (src, dst) in enumerate(pairs)]
    for copy in copies:
        copy.start()
    for copy in copies:
        copy.wait()


def column_of(row):
    n = row.shape[1]
    square = jnp.broadcast_to(row, (n, n))
    return jnp.sum(jnp.where(iota((n, n), 0) == iota((n, n), 1), square, 0.0), axis=1, keepdims=True)


NU, UPPER, LOWER, EAST, WEST, PULL, SOURCE = range(7)


def fill_table(table, transport, chemistry, evap, source_map):
    nf = chemistry.shape[0]
    nu, swirl, axial = (column_of(transport[k : k + 1]) for k in range(3))
    columns = [nu, nu - 0.5 * axial, nu + 0.5 * axial, nu - 0.5 * swirl, nu + 0.5 * swirl]
    columns.append(column_of(evap[...]))
    columns += [column_of(source_map[k : k + 1]) for k in range(source_map.shape[0])]
    columns += [chemistry[:, g : g + 1] for g in range(nf)]
    for k, column in enumerate(columns):
        table[k, :nf] = jnp.broadcast_to(column, (nf, LANES))


def spread(table, k, f, rows):
    return jnp.broadcast_to(table[k, f : f + 1], (rows, LANES))


def inner_terms(gas, table, tanh):
    nf, ca, cr, cz = gas.shape
    lane = iota((cr, cz), 1)
    row = iota((cr, cz), 0)
    chem = table.shape[0] - nf
    for f in range(nf):
        nu, upper, lower, east, west = (spread(table, k, f, cr) for k in (NU, UPPER, LOWER, EAST, WEST))
        totals = []
        for a in range(ca):
            here = gas[f, a]
            total = nu * (
                jnp.where(row == cr - 1, 0.0, pltpu.roll(here, cr - 1, 0))
                + jnp.where(row == 0, 0.0, pltpu.roll(here, 1, 0))
                - 6.0 * here
            )
            total += upper * jnp.where(lane == cz - 1, 0.0, pltpu.roll(here, cz - 1, 1))
            total += lower * jnp.where(lane == 0, 0.0, pltpu.roll(here, 1, 1))
            if a < ca - 1:
                total += east * gas[f, a + 1]
            if a > 0:
                total += west * gas[f, a - 1]
            totals.append(total)
        for g in range(nf):
            rate = spread(table, chem + g, f, cr)
            for a in range(ca):
                totals[a] += rate * tanh[g, a]
        for a in range(ca):
            yield f, a, totals[a]


def probe_all(gas, host, table, hots, probed):
    nf, ca, cr, cz = gas.shape
    slots = host.shape[1]
    width = ca * cz
    for f in range(nf):
        for a in range(ca):
            upper, lower = parts_of(gas[f, a], 2)
            table[f * cr : (f + 1) * cr, a * cz : (a + 1) * cz] = upper
            table[f * cr : (f + 1) * cr, width + a * cz : width + (a + 1) * cz] = lower
    span = cr * cz
    block = 256
    for b in range(slots // block):
        cells = host[:, b * block : (b + 1) * block]
        column = (cells // span) * cz + cells % cz
        row = (cells // cz) % cr
        hots[:, b * block : (b + 1) * block] = hot(iota((width, block), 0) == column)
        ahot = hots[:, b * block : (b + 1) * block]
        found = jnp.dot(table[:, :width], ahot, preferred_element_type=F32)
        found += jnp.dot(table[:, width:], ahot, preferred_element_type=F32)
        mask = iota((cr, block), 0) == row
        found = jnp.where(mask[None], found.reshape(nf, cr, block), 0.0)
        probed[:nf, b * block : (b + 1) * block] = jnp.sum(found, axis=1)


def react(probed, attr, live, table, nf):
    pull = jnp.sum(table[PULL, :nf, 0:1] * probed[:nf], axis=0, keepdims=True)
    sig = jax.nn.sigmoid(pull + attr[1:2])
    mdot = EVAP * attr[0:1] * sig * live
    source = table[SOURCE, :nf, 0:1] * attr[0:1]
    for k in range(1, attr.shape[0]):
        source += table[SOURCE + k, :nf, 0:1] * attr[k : k + 1]
    source = source * mdot
    rows = [attr[0:1] - DT * mdot]
    rows.append(attr[1:2] + DT * RELAX * (probed[4:5] - attr[1:2]))
    rows.append(attr[2:5] + DT * RELAX * (probed[1:4] - attr[2:5]))
    rows.append(attr[5:8])
    return rows, source


def deposit_all(source, host, hots, shapes, reach, total):
    nf, ca, cr, cz = shapes
    width = ca * cz
    block = 512 if reach % 512 == 0 else 128
    for b in range(reach // block):
        cells = host[:, b * block : (b + 1) * block]
        row = (cells // cz) % cr
        mask = iota((cr, block), 0) == row
        spread = jnp.where(mask[None], source[:nf, b * block : (b + 1) * block][:, None, :], 0.0)
        upper, lower = parts_of(spread.reshape(nf * cr, block), 2)
        ahot = hots[:, b * block : (b + 1) * block]
        part = across(upper, ahot) + across(lower, ahot)
        if b == 0:
            total[...] = part
        else:
            total[...] += part


def list_hots(lists, section, slots, lhot):
    width = lists.shape[-1]
    for d in range(2):
        names = lists[0, 0, section, d : d + 1, :].astype(F32)
        column = jnp.broadcast_to(names, (width, width)).T
        for b in range(slots // width):
            at = iota((width, width), 1).astype(F32) + float(b * width)
            lhot[d * width : (d + 1) * width, b * width : (b + 1) * width] = hot(column == at)


def gather(parcels, lhot):
    parts = jnp.concatenate(parts_of(parcels, 3), axis=0)
    taken = across(parts, lhot)
    return taken[:ROWS] + taken[ROWS : 2 * ROWS] + taken[2 * ROWS :]


def gone_from(lhot):
    ones = jnp.ones((8, lhot.shape[0]), BF16)
    return jnp.dot(ones, lhot, preferred_element_type=F32)[0:1]


def packs_of(taken, lists, section, span, slots):
    width = lists.shape[-1]
    packs = []
    for d in range(2):
        valid = lists[0, 0, section, d : d + 1, :] < slots
        pack = taken[:, d * width : (d + 1) * width]
        cell = pack[HOST : HOST + 1].astype(jnp.int32) % span
        cell = jnp.where(valid, cell.astype(F32), -1.0)
        row = iota(pack.shape, 0)
        pack = jnp.where(row == HOST, cell, jnp.where(valid & (row < HOST), pack, 0.0))
        packs.append(pack)
    left, right = packs
    flip = odd("azim") == 1
    return jnp.where(flip, left, right), jnp.where(flip, right, left)


def send_rows(gas, near, far):
    cr = gas.shape[2]
    flip = odd("radax") == 1
    for f in range(gas.shape[0]):
        low, high = gas[f, :, 0, :], gas[f, :, cr - 1, :]
        near[f] = jnp.where(flip, low, high)
        far[f] = jnp.where(flip, high, low)


def probe_one_kernel(
    count, gas, transport, chemistry, evap, source_map, lists, mass, state, host_in,
    near, far, parcels, on, off, table, hots, source, used, cells, probed, lhot,
):
    nf, ca, cr, cz = gas.shape
    slots = probed.shape[1]
    send_rows(gas, near, far)
    fill_table(table, transport, chemistry, evap, source_map)
    host = host_in[0]
    used[...] = jnp.broadcast_to(count[...].astype(F32), used.shape)
    live = (iota((1, slots), 1) < count[...]).astype(F32)
    attr = jnp.concatenate([mass[0]] + [state[k, 0] for k in range(state.shape[0])], axis=0)
    source[:nf] = parcel_work(gas, host, attr, live, table, parcels, cells, hots, probed)
    list_hots(lists, 0, slots, lhot)
    on[...], off[...] = packs_of(gather(parcels[:, :slots], lhot[...]), lists, 0, cr * cz, slots)
    parcels[LIVE : LIVE + 1, :slots] = jnp.where(gone_from(lhot[...]) > 0.5, 0.0, live)


def field_one_kernel(spare, gas, table, parcels, hots, source, out, total, tanh):
    nf, ca, cr, cz = gas.shape
    slots = hots.shape[1]
    for g in range(nf):
        tanh[g] = jnp.tanh(gas[g])
    host = parcels[HOST : HOST + 1, :slots].astype(jnp.int32)
    deposit_all(source, host, hots, gas.shape, slots - spare, total)
    for f, a, terms in inner_terms(gas, table, tanh):
        out[f, a] = gas[f, a] + DT * (terms + total[f * cr : (f + 1) * cr, a * cz : (a + 1) * cz])


def probe_two_kernel(
    gas, table, lists, old, near, far, parcels, hots, source, taken, lhot, cells, probed
):
    slots = probed.shape[1]
    send_rows(gas, near, far)
    host = old[HOST : HOST + 1, :slots].astype(jnp.int32)
    source[: gas.shape[0]] = parcel_work(
        gas, host, old[0:HOST, :slots], old[LIVE : LIVE + 1, :slots], table, parcels, cells, hots, probed
    )
    list_hots(lists, 1, slots, lhot)
    taken[...] = gather(parcels[:, :slots], lhot[...])
    parcels[GONE : GONE + 1, :slots] = gone_from(lhot[...])


def field_two_kernel(spare, gas, table, old_gas, parcels, hots, source, out, total, tanh):
    nf, ca, cr, cz = gas.shape
    slots = hots.shape[1]
    for g in range(nf):
        tanh[g] = jnp.tanh(gas[g])
    host = parcels[HOST : HOST + 1, :slots].astype(jnp.int32)
    deposit_all(source, host, hots, gas.shape, slots - spare, total)
    for f, a, terms in inner_terms(gas, table, tanh):
        terms += total[f * cr : (f + 1) * cr, a * cz : (a + 1) * cz]
        out[f, a] = 0.5 * (old_gas[f, a] + gas[f, a] + DT * terms)


def parcel_work(gas, host, attr, live, table, parcels, cells, hots, probed):
    slots = probed.shape[1]
    probe_all(gas, host, cells, hots, probed)
    rows, source = react(probed[...], attr, live, table, gas.shape[0])
    parcels[...] = jnp.zeros_like(parcels)
    parcels[0:ROWS, :slots] = jnp.concatenate(
        rows + [host.astype(F32), live, jnp.zeros((ROWS - LIVE - 1, slots), F32)], axis=0
    )
    return source


def edge_terms(scale, table, out, on, off, near, far):
    nf, ca, cr, cz = out.shape
    block = lax.axis_index("radax")
    inner, outer = block == 0, block == lax.axis_size("radax") - 1
    flip_a, flip_r = odd("azim") == 1, odd("radax") == 1
    for f in range(nf):
        got_on, got_off = on[f * cr : (f + 1) * cr], off[f * cr : (f + 1) * cr]
        east = jnp.where(flip_a, got_off, got_on)
        west = jnp.where(flip_a, got_on, got_off)
        out[f, 0] += (scale * spread(table, WEST, f, cr)) * west
        out[f, ca - 1] += (scale * spread(table, EAST, f, cr)) * east
        north = jnp.where(outer, 0.0, jnp.where(flip_r, far[f], near[f]))
        south = jnp.where(inner, 0.0, jnp.where(flip_r, near[f], far[f]))
        nu = scale * spread(table, NU, f, ca)
        out[f, :, 0, :] += nu * south
        out[f, :, cr - 1, :] += nu * north


def edge_kernel(table, base, off, on, far, near, pack_on, pack_off, out, send_on, send_off):
    nf, ca, cr, cz = out.shape
    out[...] = base[...]
    edge_terms(DT, table, out, on, off, near, far)
    flip = odd("azim") == 1
    for f in range(nf):
        low, high = out[f, 0], out[f, ca - 1]
        send_on[f * cr : (f + 1) * cr] = jnp.where(flip, low, high)
        send_off[f * cr : (f + 1) * cr] = jnp.where(flip, high, low)
    send_on[nf * cr :] = pack_on[...]
    send_off[nf * cr :] = pack_off[...]


def put(parcels, pack, start, live):
    width = pack.shape[1]
    row = iota(pack.shape, 0)
    pack = jnp.where(row == LIVE, live, pack)
    shift = start % width
    first = pl.multiple_of((start // width) * width, width)
    pack = pltpu.roll(pack, shift, 1)
    lane = iota(pack.shape, 1)
    taken = pack[LIVE : LIVE + 1] > 0.5
    here = parcels[:, pl.ds(first, width)]
    parcels[:, pl.ds(first, width)] = jnp.where(taken & (lane >= shift) & (row != GONE), pack, here)
    second = pl.multiple_of(first + width, width)
    here = parcels[:, pl.ds(second, width)]
    parcels[:, pl.ds(second, width)] = jnp.where(taken & (lane < shift) & (row != GONE), pack, here)


def sides(on, off):
    flip = odd("azim") == 1
    return jnp.where(flip, on, off), jnp.where(flip, off, on)


def scalar(ref):
    return jnp.max(ref[0:1]).astype(jnp.int32)


def arrive_kernel(
    count, gas, table, lists, on, off, old, taken, lhot, parcels, send_on, send_off, sources, used, cells
):
    nf, ca, cr, cz = gas.shape
    slots = lhot.shape[1]
    base = nf * cr
    packs = sides(on[base:], off[base:])
    parcels[...] = old[...]
    start = scalar(count)
    for side in range(2):
        layer = side * (ca - 1)
        pack = packs[side]
        cell = pack[HOST : HOST + 1].astype(jnp.int32)
        live = (cell >= 0).astype(F32)
        for f in range(nf):
            upper, lower = parts_of(gas[f, layer], 2)
            cells[f * cr : (f + 1) * cr, :cz] = upper
            cells[f * cr : (f + 1) * cr, cz:] = lower
        zhot = hot(iota((cz, cell.shape[1]), 0) == cell % cz)
        found = jnp.dot(cells[:, :cz], zhot, preferred_element_type=F32)
        found += jnp.dot(cells[:, cz:], zhot, preferred_element_type=F32)
        mask = iota((cr, cell.shape[1]), 0) == cell // cz
        found = jnp.where(mask[None], found.reshape(nf, cr, cell.shape[1]), 0.0)
        probed = jnp.sum(found, axis=1)
        rows, source = react(probed, pack[0:HOST], live, table, nf)
        sources[side, :nf] = source
        sources[side, nf : nf + 1] = pack[HOST : HOST + 1]
        home = (cell + layer * cr * cz).astype(F32)
        moved = jnp.concatenate(rows + [home, live, jnp.zeros((ROWS - LIVE - 1, cell.shape[1]), F32)], 0)
        put(parcels, moved, start, live)
        start = start + jnp.sum(live).astype(jnp.int32)
    used[...] = jnp.broadcast_to(start.astype(F32), used.shape)
    width = lists.shape[-1]
    first = pl.multiple_of(scalar(count), width)
    window = pl.ds(first, 2 * width)
    again = gather(parcels[:, window], lhot[:, window])
    names = jnp.concatenate([lists[0, 0, 1, d : d + 1, :] for d in range(2)], axis=1)
    inside = (names >= first) & (names < first + 2 * width)
    both = jnp.where(inside, again, taken[...])
    send_on[...], send_off[...] = packs_of(both, lists, 1, cr * cz, slots)
    gone = parcels[GONE : GONE + 1, :slots] > 0.5
    parcels[LIVE : LIVE + 1, :slots] = jnp.where(gone, 0.0, parcels[LIVE : LIVE + 1, :slots])


def finish_kernel(table, base, off, on, near, far, sources, out):
    nf, ca, cr, cz = out.shape
    out[...] = base[...]
    edge_terms(0.5 * DT, table, out, on, off, near, far)
    for side in range(2):
        layer = side * (ca - 1)
        cell = sources[side, nf : nf + 1].astype(jnp.int32)
        mask = iota((cr, cell.shape[1]), 0) == cell // cz
        laid = jnp.where(mask[None], sources[side, :nf][:, None, :], 0.0)
        upper, lower = parts_of(laid.reshape(nf * cr, cell.shape[1]), 2)
        zhot = hot(iota((cz, cell.shape[1]), 0) == cell % cz)
        total = across(upper, zhot) + across(lower, zhot)
        for f in range(nf):
            out[f, layer] += (0.5 * DT) * total[f * cr : (f + 1) * cr]


def place_kernel(far_offset, count, off, on, old, mass, state, host, used, parcels):
    slots = mass.shape[-1]
    parcels[...] = old[...]
    packs = sides(on[...], off[...])
    start = scalar(count)
    for side in range(2):
        pack = packs[side]
        live = (pack[HOST : HOST + 1] >= 0.0).astype(F32)
        row = iota(pack.shape, 0)
        pack = jnp.where(row == HOST, pack + float(side * far_offset), pack)
        put(parcels, pack, start, live)
        start = start + jnp.sum(live).astype(jnp.int32)
    used[...] = jnp.broadcast_to(start, (1, 1))
    live = parcels[LIVE : LIVE + 1, :slots] > 0.5
    mass[0] = jnp.where(live, parcels[0:1, :slots], 0.0)
    for k in range(state.shape[0]):
        state[k, 0] = jnp.where(live, parcels[k + 1 : k + 2, :slots], 0.0)
    host[0] = jnp.where(live, parcels[HOST : HOST + 1, :slots].astype(jnp.int32), -1)


def swap(array, axis, phase):
    size = lax.axis_size(axis)
    pairs = []
    for i in range(phase, size + phase, 2):
        j = (i + 1) % size
        pairs += [(i, j), (j, i)]
    return lax.ppermute(array, axis, pairs)


def swap_rows(array, phase):
    sectors, blocks = lax.axis_size("azim"), lax.axis_size("radax")
    pairs = []
    for i in range(sectors):
        for j in range(blocks):
            other = j + 1 if (j - phase) % 2 == 0 else j - 1
            target = (i, other) if 0 <= other < blocks else (i ^ 1, j)
            pairs.append((i * blocks + j, target[0] * blocks + target[1]))
    return lax.ppermute(array, ("azim", "radax"), pairs)


def on_device(
    gas, transport, chemistry, evap, source_map, mass, state, host, count, crossing
):
    nf, ca, cr, cz = gas.shape
    slots = mass.shape[-1]
    width = crossing.shape[-1]
    padded = slots + 2 * width
    ring, pack = shape((nf, ca, cz)), shape((ROWS, width))
    tile = shape((8, LANES))
    grid, slotted = shape(gas.shape), shape((ROWS, padded))
    small = (transport, chemistry, evap.reshape(1, nf), source_map.T, mass, state, host, crossing)
    on, off, *small = call(
        pack_kernel,
        [shape((nf, cr, cz)), shape((nf, cr, cz))] + [shape(v.shape, v.dtype) for v in small],
        [HBM] * (1 + len(small)),
        [VMEM] * (2 + len(small)),
        tuple(pltpu.with_memory_space_constraint(v, pltpu.HBM) for v in (gas,) + small),
        scratch=[pltpu.SemaphoreType.DMA((2 + len(small),))],
        flops=5_000_000_000,
        moved=2_000_000,
    )
    transport, chemistry, evap, source_map, mass, state, host, crossing = small
    off = swap(off.reshape(nf * cr, cz), "azim", 1)
    on = swap(on.reshape(nf * cr, cz), "azim", 0)

    hots, lhot = shape((ca * cz, slots), BF16), shape((2 * width, slots), BF16)
    source = shape((ROWS, slots))
    probe_scratch = [pltpu.VMEM((nf * cr, 2 * ca * cz), BF16), pltpu.VMEM((ROWS, slots), F32)]
    field_scratch = [pltpu.VMEM((nf * cr, ca * cz), F32), pltpu.VMEM(gas.shape, F32)]
    heavy = dict(flops=3_000_000_000, moved=2_000_000, trans=300_000)
    near, far, parcels, pack_on, pack_off, table, cell_hots, sources, used = call(
        probe_one_kernel,
        [ring, ring, slotted, pack, pack, shape((SOURCE + source_map.shape[0] + nf, ROWS, LANES)), hots, source, tile],
        [VMEM] * 10,
        [VMEM] * 9,
        (count, gas, transport, chemistry, evap, source_map, crossing, mass, state, host),
        scratch=probe_scratch + [pltpu.VMEM(lhot.shape, BF16)],
        **heavy,
    )
    near = swap_rows(near, 0)
    far = swap_rows(far, 1)
    base = call(
        functools.partial(field_one_kernel, 4 * width),
        grid,
        [VMEM] * 5,
        VMEM,
        (gas, table, parcels, cell_hots, sources),
        scratch=field_scratch,
        flops=1_000_000,
        moved=10_000,
    )
    longer = shape((nf * cr + ROWS, cz))
    section_one, on, off = call(
        edge_kernel,
        [grid, longer, longer],
        [VMEM] * 8,
        [VMEM] * 3,
        (table, base, off, on, far, near, pack_on, pack_off),
        aliases={1: 0},
        moved=3_000_000,
    )
    off = swap(off, "azim", 1)
    on = swap(on, "azim", 0)
    near, far, parcels, cell_hots, sources, taken, named = call(
        probe_two_kernel,
        [ring, ring, slotted, hots, source, shape((ROWS, 2 * width)), lhot],
        [VMEM] * 4,
        [VMEM] * 7,
        (section_one, table, crossing, parcels),
        scratch=probe_scratch,
        **heavy,
    )
    near = swap_rows(near, 0)
    far = swap_rows(far, 1)
    base = call(
        functools.partial(field_two_kernel, 4 * width),
        grid,
        [VMEM] * 6,
        VMEM,
        (section_one, table, gas, parcels, cell_hots, sources),
        scratch=field_scratch,
        flops=1_000_000,
        moved=10_000,
    )
    parcels, pack_on, pack_off, sources, used_now = call(
        arrive_kernel,
        [slotted, pack, pack, shape((2, ROWS, width)), tile],
        [VMEM] * 9,
        [VMEM] * 5,
        (used, section_one, table, crossing, on, off, parcels, taken, named),
        scratch=[pltpu.VMEM((nf * cr, 2 * cz), BF16)],
        flops=100_000_000,
        moved=2_000_000,
    )
    pack_off = swap(pack_off, "azim", 1)
    pack_on = swap(pack_on, "azim", 0)
    gas_next = call(
        finish_kernel,
        shape(gas.shape),
        [VMEM] * 7,
        VMEM,
        (table, base, off, on, near, far, sources),
        flops=100_000_000,
        moved=3_000_000,
    )
    mass_next, state_next, host_next, count_next = call(
        functools.partial(place_kernel, (ca - 1) * cr * cz),
        [shape(mass.shape), shape(state.shape), shape(host.shape, jnp.int32), shape((1, 1), jnp.int32)],
        [VMEM] * 4,
        [VMEM] * 4,
        (used_now, pack_off, pack_on, parcels),
        scratch=[pltpu.VMEM((ROWS, padded), F32)],
        moved=500_000,
    )
    return gas_next, mass_next, state_next, host_next, count_next


def solution(mesh):
    in_specs = (
        P(None, "azim", "radax", None),
        P(),
        P(),
        P(),
        P(),
        P("azim", "radax", None),
        P(None, "azim", "radax", None),
        P("azim", "radax", None),
        P("azim", "radax"),
        P("azim", "radax", None, None, None),
    )
    out_specs = (
        P(None, "azim", "radax", None),
        P("azim", "radax", None),
        P(None, "azim", "radax", None),
        P("azim", "radax", None),
        P("azim", "radax"),
    )
    return jax.shard_map(
        on_device, mesh=mesh, in_specs=in_specs, out_specs=out_specs, check_vma=False
    )
```

```python
import functools

import jax
import jax.numpy as jnp
from jax import lax
from jax.experimental import pallas as pl
from jax.experimental.pallas import tpu as pltpu
from jax.sharding import PartitionSpec as P

DT = 0.5
RELAX = 0.3
EVAP = 0.5
F32 = jnp.float32
BF16 = jnp.bfloat16
ROWS = 16
HOST = 8
LIVE = 9
GONE = 10
LANES = 128
LIMIT = 40 << 20

VMEM = pl.BlockSpec(memory_space=pltpu.VMEM)
HBM = pl.BlockSpec(memory_space=pltpu.HBM)


def iota(shape, dim, dtype=jnp.int32):
    return lax.broadcasted_iota(dtype, shape, dim)


def parts_of(values, count):
    parts = []
    for _ in range(count - 1):
        part = values.astype(BF16)
        parts.append(part)
        values = values - part.astype(F32)
    return parts + [values.astype(BF16)]


def hot(mask):
    return mask.astype(F32).astype(BF16)


def across(left, right):
    return lax.dot_general(left, right, (((1,), (1,)), ((), ())), preferred_element_type=F32)


def call(kernel, outs, ins, out_specs, args, scratch=(), aliases=None, flops=0, moved=0, trans=0):
    return pl.pallas_call(
        kernel,
        out_shape=outs,
        in_specs=ins,
        out_specs=out_specs,
        scratch_shapes=list(scratch),
        input_output_aliases=aliases or {},
        compiler_params=pltpu.CompilerParams(vmem_limit_bytes=LIMIT),
        cost_estimate=pl.CostEstimate(flops=flops, bytes_accessed=moved, transcendentals=trans),
    )(*args)


def shape(dims, dtype=F32):
    return jax.ShapeDtypeStruct(dims, dtype)


def odd(axis):
    return lax.axis_index(axis) % 2


def pack_kernel(gas, *refs):
    small = (len(refs) - 3) // 2
    sources, (on, off), targets = refs[:small], refs[small : small + 2], refs[small + 2 : -1]
    sems = refs[-1]
    last = gas.shape[1] - 1
    flip = odd("azim")
    pairs = [(gas.at[:, last * flip], off), (gas.at[:, last * (1 - flip)], on)]
    pairs += list(zip(sources, targets))
    copies = [pltpu.make_async_copy(src, dst, sems.at[k]) for k, (src, dst) in enumerate(pairs)]
    for copy in copies:
        copy.start()
    for copy in copies:
        copy.wait()


def column_of(row):
    n = row.shape[1]
    square = jnp.broadcast_to(row, (n, n))
    return jnp.sum(jnp.where(iota((n, n), 0) == iota((n, n), 1), square, 0.0), axis=1, keepdims=True)


NU, UPPER, LOWER, EAST, WEST, PULL, SOURCE = range(7)


def fill_table(table, transport, chemistry, evap, source_map):
    nf = chemistry.shape[0]
    nu, swirl, axial = (column_of(transport[k : k + 1]) for k in range(3))
    columns = [nu, nu - 0.5 * axial, nu + 0.5 * axial, nu - 0.5 * swirl, nu + 0.5 * swirl]
    columns.append(column_of(evap[...]))
    columns += [column_of(source_map[k : k + 1]) for k in range(source_map.shape[0])]
    columns += [chemistry[:, g : g + 1] for g in range(nf)]
    for k, column in enumerate(columns):
        table[k, :nf] = jnp.broadcast_to(column, (nf, LANES))


def spread(table, k, f, rows):
    return jnp.broadcast_to(table[k, f : f + 1], (rows, LANES))


def inner_terms(gas, table, tanh, layers):
    nf, ca, cr, cz = gas.shape
    lane = iota((cr, cz), 1)
    row = iota((cr, cz), 0)
    chem = table.shape[0] - nf
    for g in range(nf):
        for a in layers:
            tanh[g, a] = jnp.tanh(gas[g, a])
    for f in range(nf):
        nu, upper, lower, east, west = (spread(table, k, f, cr) for k in (NU, UPPER, LOWER, EAST, WEST))
        totals = {}
        for a in layers:
            here = gas[f, a]
            total = nu * (
                jnp.where(row == cr - 1, 0.0, pltpu.roll(here, cr - 1, 0))
                + jnp.where(row == 0, 0.0, pltpu.roll(here, 1, 0))
                - 6.0 * here
            )
            total += upper * jnp.where(lane == cz - 1, 0.0, pltpu.roll(here, cz - 1, 1))
            total += lower * jnp.where(lane == 0, 0.0, pltpu.roll(here, 1, 1))
            if a < ca - 1:
                total += east * gas[f, a + 1]
            if a > 0:
                total += west * gas[f, a - 1]
            totals[a] = total
        for g in range(nf):
            rate = spread(table, chem + g, f, cr)
            for a in layers:
                totals[a] += rate * tanh[g, a]
        for a in layers:
            yield f, a, totals[a]


def probe_all(gas, host, table, hots, probed):
    nf, ca, cr, cz = gas.shape
    slots = host.shape[1]
    width = ca * cz
    for f in range(nf):
        for a in range(ca):
            upper, lower = parts_of(gas[f, a], 2)
            table[f * cr : (f + 1) * cr, a * cz : (a + 1) * cz] = upper
            table[f * cr : (f + 1) * cr, width + a * cz : width + (a + 1) * cz] = lower
    span = cr * cz
    block = 256

    def probe(b):
        cells = host[:, b * block : (b + 1) * block]
        column = (cells // span) * cz + cells % cz
        row = (cells // cz) % cr
        hots[:, b * block : (b + 1) * block] = hot(iota((width, block), 0) == column)
        ahot = hots[:, b * block : (b + 1) * block]
        found = jnp.dot(table[:, :width], ahot, preferred_element_type=F32)
        found += jnp.dot(table[:, width:], ahot, preferred_element_type=F32)
        mask = iota((cr, block), 0) == row
        found = jnp.where(mask[None], found.reshape(nf, cr, block), 0.0)
        probed[:nf, b * block : (b + 1) * block] = jnp.sum(found, axis=1)

    for b in range(slots // block):
        probe(b)


def react(probed, attr, live, table, nf):
    pull = jnp.sum(table[PULL, :nf, 0:1] * probed[:nf], axis=0, keepdims=True)
    sig = jax.nn.sigmoid(pull + attr[1:2])
    mdot = EVAP * attr[0:1] * sig * live
    source = table[SOURCE, :nf, 0:1] * attr[0:1]
    for k in range(1, attr.shape[0]):
        source += table[SOURCE + k, :nf, 0:1] * attr[k : k + 1]
    source = source * mdot
    rows = [attr[0:1] - DT * mdot]
    rows.append(attr[1:2] + DT * RELAX * (probed[4:5] - attr[1:2]))
    rows.append(attr[2:5] + DT * RELAX * (probed[1:4] - attr[2:5]))
    rows.append(attr[5:8])
    return rows, source


def deposit_all(source, host, hots, shapes, reach, total):
    nf, ca, cr, cz = shapes
    block = 512 if reach % 512 == 0 else 128
    for b in range(reach // block):
        cells = host[:, b * block : (b + 1) * block]
        row = (cells // cz) % cr
        mask = iota((cr, block), 0) == row
        ahot = hots[:, b * block : (b + 1) * block]
        part = None
        for piece in parts_of(source[:nf, b * block : (b + 1) * block], 2):
            piece = piece.astype(F32)
            laid = [jnp.where(mask, piece[f : f + 1], 0.0).astype(BF16) for f in range(nf)]
            one = across(jnp.concatenate(laid, axis=0), ahot)
            part = one if part is None else part + one
        if b == 0:
            total[...] = part
        else:
            total[...] += part


def list_hots(lists, section, slots, lhot):
    width = lists.shape[-1]
    for d in range(2):
        names = lists[0, 0, section, d : d + 1, :].astype(F32)
        column = jnp.broadcast_to(names, (width, width)).T
        for b in range(slots // width):
            at = iota((width, width), 1).astype(F32) + float(b * width)
            lhot[d * width : (d + 1) * width, b * width : (b + 1) * width] = hot(column == at)


def gather(parcels, lhot):
    parts = jnp.concatenate(parts_of(parcels, 3), axis=0)
    taken = across(parts, lhot)
    return taken[:ROWS] + taken[ROWS : 2 * ROWS] + taken[2 * ROWS :]


def gone_from(lhot):
    ones = jnp.ones((8, lhot.shape[0]), BF16)
    return jnp.dot(ones, lhot, preferred_element_type=F32)[0:1]


def packs_of(taken, lists, section, span, slots):
    width = lists.shape[-1]
    packs = []
    for d in range(2):
        valid = lists[0, 0, section, d : d + 1, :] < slots
        pack = taken[:, d * width : (d + 1) * width]
        cell = pack[HOST : HOST + 1].astype(jnp.int32) % span
        cell = jnp.where(valid, cell.astype(F32), -1.0)
        row = iota(pack.shape, 0)
        pack = jnp.where(row == HOST, cell, jnp.where(valid & (row < HOST), pack, 0.0))
        packs.append(pack)
    left, right = packs
    flip = odd("azim") == 1
    return jnp.where(flip, left, right), jnp.where(flip, right, left)


def rows_kernel(gas, after, near, far):
    send_rows(gas, near, far)


def send_rows(gas, near, far):
    cr = gas.shape[2]
    flip = odd("radax") == 1
    for f in range(gas.shape[0]):
        low, high = gas[f, :, 0, :], gas[f, :, cr - 1, :]
        near[f] = jnp.where(flip, low, high)
        far[f] = jnp.where(flip, high, low)


def probe_one_kernel(
    count, gas, transport, chemistry, evap, source_map, lists, mass, state, host_in,
    parcels, on, off, table, hots, source, used, cells, probed, lhot,
):
    nf, ca, cr, cz = gas.shape
    slots = probed.shape[1]
    fill_table(table, transport, chemistry, evap, source_map)
    host = host_in[0]
    used[...] = jnp.broadcast_to(count[...].astype(F32), used.shape)
    live = (iota((1, slots), 1) < count[...]).astype(F32)
    attr = jnp.concatenate([mass[0]] + [state[k, 0] for k in range(state.shape[0])], axis=0)
    source[:nf] = parcel_work(gas, host, attr, live, table, parcels, cells, hots, probed)
    list_hots(lists, 0, slots, lhot)
    on[...], off[...] = packs_of(gather(parcels[:, :slots], lhot[...]), lists, 0, cr * cz, slots)
    parcels[LIVE : LIVE + 1, :slots] = jnp.where(gone_from(lhot[...]) > 0.5, 0.0, live)


def field_one_kernel(reach, gas, table, parcels, hots, source, out, total, tanh):
    nf, ca, cr, cz = gas.shape
    host = parcels[HOST : HOST + 1, :reach].astype(jnp.int32)
    deposit_all(source, host, hots, gas.shape, reach, total)
    for f, a, terms in inner_terms(gas, table, tanh, (0, ca - 1)):
        terms += total[f * cr : (f + 1) * cr, a * cz : (a + 1) * cz]
        out[f, min(a, 1)] = gas[f, a] + DT * terms


def radial_halos(near, far, f):
    block = lax.axis_index("radax")
    flip = odd("radax") == 1
    north = jnp.where(flip, far[f], near[f])
    south = jnp.where(flip, near[f], far[f])
    return jnp.where(block == 0, 0.0, south), jnp.where(block == lax.axis_size("radax") - 1, 0.0, north)


def edge_kernel(table, outer, far, near, pack_on, pack_off, send_on, send_off):
    nf, _, cr, cz = outer.shape
    ca = near.shape[1]
    flip = odd("azim") == 1
    row = iota((cr, cz), 0)
    for f in range(nf):
        south, north = radial_halos(near, far, f)
        nu = DT * spread(table, NU, f, cr)
        low, high = (
            outer[f, k]
            + nu
            * (
                jnp.where(row == 0, jnp.broadcast_to(south[a : a + 1], (cr, cz)), 0.0)
                + jnp.where(row == cr - 1, jnp.broadcast_to(north[a : a + 1], (cr, cz)), 0.0)
            )
            for k, a in ((0, 0), (1, ca - 1))
        )
        send_on[f * cr : (f + 1) * cr] = jnp.where(flip, low, high)
        send_off[f * cr : (f + 1) * cr] = jnp.where(flip, high, low)
    send_on[nf * cr :] = pack_on[...]
    send_off[nf * cr :] = pack_off[...]


def join_kernel(gas, table, outer, total, off, on, far, near, out, tanh):
    nf, ca, cr, cz = gas.shape
    for f in range(nf):
        out[f, 0] = outer[f, 0]
        out[f, ca - 1] = outer[f, 1]
    for f, a, terms in inner_terms(gas, table, tanh, range(1, ca - 1)):
        terms += total[f * cr : (f + 1) * cr, a * cz : (a + 1) * cz]
        out[f, a] = gas[f, a] + DT * terms
    for f in range(nf):
        west, east = sides(on[f * cr : (f + 1) * cr], off[f * cr : (f + 1) * cr])
        edge_terms(DT, table, out, f, west, east, near, far)


def probe_two_kernel(
    gas, table, lists, old, near, far, parcels, hots, source, taken, lhot, cells, probed
):
    slots = probed.shape[1]
    send_rows(gas, near, far)
    host = old[HOST : HOST + 1, :slots].astype(jnp.int32)
    live = old[LIVE : LIVE + 1, :slots]
    source[: gas.shape[0]] = parcel_work(
        gas, host, old[0:HOST, :slots], live, table, parcels, cells, hots, probed
    )
    list_hots(lists, 1, slots, lhot)
    taken[...] = gather(parcels[:, :slots], lhot[...])
    parcels[GONE : GONE + 1, :slots] = gone_from(lhot[...])


def field_two_kernel(reach, gas, table, old_gas, parcels, hots, source, out, total, tanh):
    nf, ca, cr, cz = gas.shape
    host = parcels[HOST : HOST + 1, :reach].astype(jnp.int32)
    deposit_all(source, host, hots, gas.shape, reach, total)
    for f, a, terms in inner_terms(gas, table, tanh, range(ca)):
        terms += total[f * cr : (f + 1) * cr, a * cz : (a + 1) * cz]
        out[f, a] = 0.5 * (old_gas[f, a] + gas[f, a] + DT * terms)


def parcel_work(gas, host, attr, live, table, parcels, cells, hots, probed):
    slots = probed.shape[1]
    probe_all(gas, host, cells, hots, probed)
    rows, source = react(probed[...], attr, live, table, gas.shape[0])
    parcels[...] = jnp.zeros_like(parcels)
    parcels[0:ROWS, :slots] = jnp.concatenate(
        rows + [host.astype(F32), live, jnp.zeros((ROWS - LIVE - 1, slots), F32)], axis=0
    )
    return source


def edge_terms(scale, table, out, f, west, east, near, far):
    ca, cr = out.shape[1], out.shape[2]
    out[f, 0] += (scale * spread(table, WEST, f, cr)) * west
    out[f, ca - 1] += (scale * spread(table, EAST, f, cr)) * east
    south, north = radial_halos(near, far, f)
    nu = scale * spread(table, NU, f, ca)
    out[f, :, 0, :] += nu * south
    out[f, :, cr - 1, :] += nu * north


def put(parcels, pack, start, live):
    width = pack.shape[1]
    row = iota(pack.shape, 0)
    pack = jnp.where(row == LIVE, live, pack)
    shift = start % width
    first = pl.multiple_of((start // width) * width, width)
    pack = pltpu.roll(pack, shift, 1)
    lane = iota(pack.shape, 1)
    taken = pack[LIVE : LIVE + 1] > 0.5
    here = parcels[:, pl.ds(first, width)]
    parcels[:, pl.ds(first, width)] = jnp.where(taken & (lane >= shift) & (row != GONE), pack, here)
    second = pl.multiple_of(first + width, width)
    here = parcels[:, pl.ds(second, width)]
    parcels[:, pl.ds(second, width)] = jnp.where(taken & (lane < shift) & (row != GONE), pack, here)


def sides(on, off):
    flip = odd("azim") == 1
    return jnp.where(flip, on, off), jnp.where(flip, off, on)


def scalar(ref):
    return jnp.max(ref[0:1]).astype(jnp.int32)


def arrive_kernel(
    count, gas, table, lists, on, off, old, taken, lhot, parcels, send_on, send_off, sources, used, cells
):
    nf, ca, cr, cz = gas.shape
    slots = lhot.shape[1]
    base = nf * cr
    packs = sides(on[base:], off[base:])
    parcels[...] = old[...]
    start = scalar(count)
    for side in range(2):
        layer = side * (ca - 1)
        pack = packs[side]
        cell = pack[HOST : HOST + 1].astype(jnp.int32)
        live = (cell >= 0).astype(F32)
        for f in range(nf):
            upper, lower = parts_of(gas[f, layer], 2)
            cells[f * cr : (f + 1) * cr, :cz] = upper
            cells[f * cr : (f + 1) * cr, cz:] = lower
        zhot = hot(iota((cz, cell.shape[1]), 0) == cell % cz)
        found = jnp.dot(cells[:, :cz], zhot, preferred_element_type=F32)
        found += jnp.dot(cells[:, cz:], zhot, preferred_element_type=F32)
        mask = iota((cr, cell.shape[1]), 0) == cell // cz
        found = jnp.where(mask[None], found.reshape(nf, cr, cell.shape[1]), 0.0)
        probed = jnp.sum(found, axis=1)
        rows, source = react(probed, pack[0:HOST], live, table, nf)
        sources[side, :nf] = source
        sources[side, nf : nf + 1] = pack[HOST : HOST + 1]
        home = (cell + layer * cr * cz).astype(F32)
        moved = jnp.concatenate(rows + [home, live, jnp.zeros((ROWS - LIVE - 1, cell.shape[1]), F32)], 0)
        put(parcels, moved, start, live)
        start = start + jnp.sum(live).astype(jnp.int32)
    used[...] = jnp.broadcast_to(start.astype(F32), used.shape)
    width = lists.shape[-1]
    first = pl.multiple_of(scalar(count), width)
    window = pl.ds(first, 2 * width)
    again = gather(parcels[:, window], lhot[:, window])
    names = jnp.concatenate([lists[0, 0, 1, d : d + 1, :] for d in range(2)], axis=1)
    inside = (names >= first) & (names < first + 2 * width)
    both = jnp.where(inside, again, taken[...])
    send_on[...], send_off[...] = packs_of(both, lists, 1, cr * cz, slots)
    gone = parcels[GONE : GONE + 1, :slots] > 0.5
    parcels[LIVE : LIVE + 1, :slots] = jnp.where(gone, 0.0, parcels[LIVE : LIVE + 1, :slots])


def finish_kernel(table, base, gas, off, on, near, far, sources, out):
    nf, ca, cr, cz = out.shape
    out[...] = base[...]
    for f in range(nf):
        west, east = sides(on[f * cr : (f + 1) * cr], off[f * cr : (f + 1) * cr])
        west += (DT * spread(table, EAST, f, cr)) * gas[f, 0]
        east += (DT * spread(table, WEST, f, cr)) * gas[f, ca - 1]
        edge_terms(0.5 * DT, table, out, f, west, east, near, far)
    for side in range(2):
        layer = side * (ca - 1)
        cell = sources[side, nf : nf + 1].astype(jnp.int32)
        mask = iota((cr, cell.shape[1]), 0) == cell // cz
        laid = jnp.where(mask[None], sources[side, :nf][:, None, :], 0.0)
        upper, lower = parts_of(laid.reshape(nf * cr, cell.shape[1]), 2)
        zhot = hot(iota((cz, cell.shape[1]), 0) == cell % cz)
        total = across(upper, zhot) + across(lower, zhot)
        for f in range(nf):
            out[f, layer] += (0.5 * DT) * total[f * cr : (f + 1) * cr]


def place_kernel(far_offset, count, off, on, old, mass, state, host, used, parcels):
    slots = mass.shape[-1]
    parcels[...] = old[...]
    packs = sides(on[...], off[...])
    start = scalar(count)
    for side in range(2):
        pack = packs[side]
        live = (pack[HOST : HOST + 1] >= 0.0).astype(F32)
        row = iota(pack.shape, 0)
        pack = jnp.where(row == HOST, pack + float(side * far_offset), pack)
        put(parcels, pack, start, live)
        start = start + jnp.sum(live).astype(jnp.int32)
    used[...] = jnp.broadcast_to(start, (1, 1))
    live = parcels[LIVE : LIVE + 1, :slots] > 0.5
    mass[0] = jnp.where(live, parcels[0:1, :slots], 0.0)
    for k in range(state.shape[0]):
        state[k, 0] = jnp.where(live, parcels[k + 1 : k + 2, :slots], 0.0)
    host[0] = jnp.where(live, parcels[HOST : HOST + 1, :slots].astype(jnp.int32), -1)


def swap(array, axis, phase):
    size = lax.axis_size(axis)
    pairs = []
    for i in range(phase, size + phase, 2):
        j = (i + 1) % size
        pairs += [(i, j), (j, i)]
    return lax.ppermute(array, axis, pairs)


def swap_rows(array, phase):
    sectors, blocks = lax.axis_size("azim"), lax.axis_size("radax")
    pairs = []
    for i in range(sectors):
        for j in range(blocks):
            other = j + 1 if (j - phase) % 2 == 0 else j - 1
            target = (i, other) if 0 <= other < blocks else (i ^ 1, j)
            pairs.append((i * blocks + j, target[0] * blocks + target[1]))
    return lax.ppermute(array, ("azim", "radax"), pairs)


def on_device(
    gas, transport, chemistry, evap, source_map, mass, state, host, count, crossing
):
    nf, ca, cr, cz = gas.shape
    slots = mass.shape[-1]
    width = crossing.shape[-1]
    padded = slots + 2 * width
    ring, pack = shape((nf, ca, cz)), shape((ROWS, width))
    tile = shape((8, LANES))
    grid, slotted = shape(gas.shape), shape((ROWS, padded))
    small = (transport, chemistry, evap.reshape(1, nf), source_map.T, mass, state, host, crossing)
    on, off, *small = call(
        pack_kernel,
        [shape((nf, cr, cz)), shape((nf, cr, cz))] + [shape(v.shape, v.dtype) for v in small],
        [HBM] * (1 + len(small)),
        [VMEM] * (2 + len(small)),
        tuple(pltpu.with_memory_space_constraint(v, pltpu.HBM) for v in (gas,) + small),
        scratch=[pltpu.SemaphoreType.DMA((2 + len(small),))],
        flops=5_000_000_000,
        moved=2_000_000,
    )
    transport, chemistry, evap, source_map, mass, state, host, crossing = small
    off = swap(off.reshape(nf * cr, cz), "azim", 1)
    on = swap(on.reshape(nf * cr, cz), "azim", 0)

    near, far = call(rows_kernel, [ring, ring], [VMEM] * 2, [VMEM] * 2, (gas, transport), moved=100_000)
    near = swap_rows(near, 0)
    far = swap_rows(far, 1)
    hots, lhot = shape((ca * cz, slots), BF16), shape((2 * width, slots), BF16)
    source = shape((ROWS, slots))
    probe_scratch = [pltpu.VMEM((nf * cr, 2 * ca * cz), BF16), pltpu.VMEM((ROWS, slots), F32)]
    tanh_scratch = pltpu.VMEM(gas.shape, F32)
    total = shape((nf * cr, ca * cz))
    heavy = dict(flops=3_000_000_000, moved=2_000_000, trans=300_000)
    light = dict(flops=1_000_000, moved=10_000)
    parcels, pack_on, pack_off, table, cell_hots, sources, used = call(
        probe_one_kernel,
        [slotted, pack, pack, shape((SOURCE + source_map.shape[0] + nf, ROWS, LANES)), hots, source, tile],
        [VMEM] * 10,
        [VMEM] * 7,
        (count, gas, transport, chemistry, evap, source_map, crossing, mass, state, host),
        scratch=probe_scratch + [pltpu.VMEM(lhot.shape, BF16)],
        **heavy,
    )
    outer, total = call(
        functools.partial(field_one_kernel, slots - 4 * width),
        [shape((nf, 2, cr, cz)), total],
        [VMEM] * 5,
        [VMEM] * 2,
        (gas, table, parcels, cell_hots, sources),
        scratch=[tanh_scratch],
        **light,
    )
    longer = shape((nf * cr + ROWS, cz))
    send_on, send_off = call(
        edge_kernel,
        [longer, longer],
        [VMEM] * 6,
        [VMEM] * 2,
        (table, outer, far, near, pack_on, pack_off),
        **light,
    )
    section_one = call(
        join_kernel,
        grid,
        [VMEM] * 8,
        VMEM,
        (gas, table, outer, total, off, on, far, near),
        scratch=[tanh_scratch],
        **heavy,
    )
    off = swap(send_off, "azim", 1)
    on = swap(send_on, "azim", 0)
    near, far, parcels, cell_hots, sources, taken, named = call(
        probe_two_kernel,
        [ring, ring, slotted, hots, source, shape((ROWS, 2 * width)), lhot],
        [VMEM] * 4,
        [VMEM] * 7,
        (section_one, table, crossing, parcels),
        scratch=probe_scratch,
        **light,
    )
    near = swap_rows(near, 0)
    far = swap_rows(far, 1)
    base = call(
        functools.partial(field_two_kernel, slots - 4 * width),
        grid,
        [VMEM] * 6,
        VMEM,
        (section_one, table, gas, parcels, cell_hots, sources),
        scratch=[pltpu.VMEM(total.shape, F32), tanh_scratch],
        **light,
    )
    parcels, pack_on, pack_off, sources, used_now = call(
        arrive_kernel,
        [slotted, pack, pack, shape((2, ROWS, width)), tile],
        [VMEM] * 9,
        [VMEM] * 5,
        (used, section_one, table, crossing, on, off, parcels, taken, named),
        scratch=[pltpu.VMEM((nf * cr, 2 * cz), BF16)],
        flops=100_000_000,
        moved=2_000_000,
    )
    pack_off = swap(pack_off, "azim", 1)
    pack_on = swap(pack_on, "azim", 0)
    gas_next = call(
        finish_kernel,
        shape(gas.shape),
        [VMEM] * 8,
        VMEM,
        (table, base, gas, off, on, near, far, sources),
        flops=100_000_000,
        moved=3_000_000,
    )
    mass_next, state_next, host_next, count_next = call(
        functools.partial(place_kernel, (ca - 1) * cr * cz),
        [shape(mass.shape), shape(state.shape), shape(host.shape, jnp.int32), shape((1, 1), jnp.int32)],
        [VMEM] * 4,
        [VMEM] * 4,
        (used_now, pack_off, pack_on, parcels),
        scratch=[pltpu.VMEM((ROWS, padded), F32)],
        moved=500_000,
    )
    return gas_next, mass_next, state_next, host_next, count_next


def solution(mesh):
    in_specs = (
        P(None, "azim", "radax", None),
        P(),
        P(),
        P(),
        P(),
        P("azim", "radax", None),
        P(None, "azim", "radax", None),
        P("azim", "radax", None),
        P("azim", "radax"),
        P("azim", "radax", None, None, None),
    )
    out_specs = (
        P(None, "azim", "radax", None),
        P("azim", "radax", None),
        P(None, "azim", "radax", None),
        P("azim", "radax", None),
        P("azim", "radax"),
    )
    return jax.shard_map(
        on_device, mesh=mesh, in_specs=in_specs, out_specs=out_specs, check_vma=False
    )
```

```python
import functools

import jax
import jax.numpy as jnp
from jax import lax
from jax.experimental import pallas as pl
from jax.experimental.pallas import tpu as pltpu
from jax.sharding import PartitionSpec as P

DT = 0.5
RELAX = 0.3
EVAP = 0.5
F32 = jnp.float32
BF16 = jnp.bfloat16
ROWS = 16
HOST = 8
LIVE = 9
GONE = 10
LANES = 128
LIMIT = 40 << 20

VMEM = pl.BlockSpec(memory_space=pltpu.VMEM)
HBM = pl.BlockSpec(memory_space=pltpu.HBM)


def iota(shape, dim, dtype=jnp.int32):
    return lax.broadcasted_iota(dtype, shape, dim)


def parts_of(values, count):
    parts = []
    for _ in range(count - 1):
        part = values.astype(BF16)
        parts.append(part)
        values = values - part.astype(F32)
    return parts + [values.astype(BF16)]


def hot(mask):
    return mask.astype(F32).astype(BF16)


def across(left, right):
    return lax.dot_general(left, right, (((1,), (1,)), ((), ())), preferred_element_type=F32)


def call(kernel, outs, ins, out_specs, args, scratch=(), aliases=None, flops=0, moved=0, trans=0):
    return pl.pallas_call(
        kernel,
        out_shape=outs,
        in_specs=ins,
        out_specs=out_specs,
        scratch_shapes=list(scratch),
        input_output_aliases=aliases or {},
        compiler_params=pltpu.CompilerParams(vmem_limit_bytes=LIMIT),
        cost_estimate=pl.CostEstimate(flops=flops, bytes_accessed=moved, transcendentals=trans),
    )(*args)


def shape(dims, dtype=F32):
    return jax.ShapeDtypeStruct(dims, dtype)


def odd(axis):
    return lax.axis_index(axis) % 2


def pack_kernel(gas, off, on, sems):
    last = gas.shape[1] - 1
    flip = odd("azim")
    pairs = [(gas.at[:, last * flip], off), (gas.at[:, last * (1 - flip)], on)]
    copies = [pltpu.make_async_copy(src, dst, sems.at[k]) for k, (src, dst) in enumerate(pairs)]
    for copy in copies:
        copy.start()
    for copy in copies:
        copy.wait()


def column_of(row):
    n = row.shape[1]
    square = jnp.broadcast_to(row, (n, n))
    return jnp.sum(jnp.where(iota((n, n), 0) == iota((n, n), 1), square, 0.0), axis=1, keepdims=True)


NU, UPPER, LOWER, EAST, WEST, PULL, SOURCE = range(7)


def fill_table(table, transport, chemistry, evap, source_map):
    nf = chemistry.shape[0]
    nu, swirl, axial = (column_of(transport[k : k + 1]) for k in range(3))
    columns = [nu, nu - 0.5 * axial, nu + 0.5 * axial, nu - 0.5 * swirl, nu + 0.5 * swirl]
    columns.append(column_of(evap[...]))
    columns += [column_of(source_map[k : k + 1]) for k in range(source_map.shape[0])]
    columns += [chemistry[:, g : g + 1] for g in range(nf)]
    for k, column in enumerate(columns):
        table[k, :nf] = jnp.broadcast_to(column, (nf, LANES))


def spread(table, k, f, rows):
    return jnp.broadcast_to(table[k, f : f + 1], (rows, LANES))


def inner_terms(gas, table, tanh, layers):
    nf, ca, cr, cz = gas.shape
    lane = iota((cr, cz), 1)
    row = iota((cr, cz), 0)
    chem = table.shape[0] - nf
    for g in range(nf):
        for a in layers:
            tanh[g, a] = jnp.tanh(gas[g, a])
    for f in range(nf):
        nu, upper, lower, east, west = (spread(table, k, f, cr) for k in (NU, UPPER, LOWER, EAST, WEST))
        totals = {}
        for a in layers:
            here = gas[f, a]
            total = nu * (
                jnp.where(row == cr - 1, 0.0, pltpu.roll(here, cr - 1, 0))
                + jnp.where(row == 0, 0.0, pltpu.roll(here, 1, 0))
                - 6.0 * here
            )
            total += upper * jnp.where(lane == cz - 1, 0.0, pltpu.roll(here, cz - 1, 1))
            total += lower * jnp.where(lane == 0, 0.0, pltpu.roll(here, 1, 1))
            if a < ca - 1:
                total += east * gas[f, a + 1]
            if a > 0:
                total += west * gas[f, a - 1]
            totals[a] = total
        for g in range(nf):
            rate = spread(table, chem + g, f, cr)
            for a in layers:
                totals[a] += rate * tanh[g, a]
        for a in layers:
            yield f, a, totals[a]


def probe_all(gas, host, table, hots, probed):
    nf, ca, cr, cz = gas.shape
    slots = host.shape[1]
    width = ca * cz
    for f in range(nf):
        for a in range(ca):
            upper, lower = parts_of(gas[f, a], 2)
            table[f * cr : (f + 1) * cr, a * cz : (a + 1) * cz] = upper
            table[f * cr : (f + 1) * cr, width + a * cz : width + (a + 1) * cz] = lower
    span = cr * cz
    block = 256

    def probe(b):
        cells = host[:, b * block : (b + 1) * block]
        column = (cells // span) * cz + cells % cz
        row = (cells // cz) % cr
        hots[:, b * block : (b + 1) * block] = hot(iota((width, block), 0) == column)
        ahot = hots[:, b * block : (b + 1) * block]
        found = jnp.dot(table[:, :width], ahot, preferred_element_type=F32)
        found += jnp.dot(table[:, width:], ahot, preferred_element_type=F32)
        mask = iota((cr, block), 0) == row
        found = jnp.where(mask[None], found.reshape(nf, cr, block), 0.0)
        probed[:nf, b * block : (b + 1) * block] = jnp.sum(found, axis=1)

    for b in range(slots // block):
        probe(b)


def react(probed, attr, live, table, nf):
    pull = jnp.sum(table[PULL, :nf, 0:1] * probed[:nf], axis=0, keepdims=True)
    sig = jax.nn.sigmoid(pull + attr[1:2])
    mdot = EVAP * attr[0:1] * sig * live
    source = table[SOURCE, :nf, 0:1] * attr[0:1]
    for k in range(1, attr.shape[0]):
        source += table[SOURCE + k, :nf, 0:1] * attr[k : k + 1]
    source = source * mdot
    rows = [attr[0:1] - DT * mdot]
    rows.append(attr[1:2] + DT * RELAX * (probed[4:5] - attr[1:2]))
    rows.append(attr[2:5] + DT * RELAX * (probed[1:4] - attr[2:5]))
    rows.append(attr[5:8])
    return rows, source


def deposit_all(source, host, hots, shapes, reach, total):
    nf, ca, cr, cz = shapes
    block = 512 if reach % 512 == 0 else 128
    for b in range(reach // block):
        cells = host[:, b * block : (b + 1) * block]
        row = (cells // cz) % cr
        mask = iota((cr, block), 0) == row
        ahot = hots[:, b * block : (b + 1) * block]
        part = None
        for piece in parts_of(source[:nf, b * block : (b + 1) * block], 2):
            piece = piece.astype(F32)
            laid = [jnp.where(mask, piece[f : f + 1], 0.0).astype(BF16) for f in range(nf)]
            one = across(jnp.concatenate(laid, axis=0), ahot)
            part = one if part is None else part + one
        if b == 0:
            total[...] = part
        else:
            total[...] += part


def list_hots(lists, section, slots, lhot):
    width = lists.shape[-1]
    for d in range(2):
        names = lists[0, 0, section, d : d + 1, :].astype(F32)
        column = jnp.broadcast_to(names, (width, width)).T
        for b in range(slots // width):
            at = iota((width, width), 1).astype(F32) + float(b * width)
            lhot[d * width : (d + 1) * width, b * width : (b + 1) * width] = hot(column == at)


def gather(parcels, lhot):
    parts = jnp.concatenate(parts_of(parcels, 3), axis=0)
    taken = across(parts, lhot)
    return taken[:ROWS] + taken[ROWS : 2 * ROWS] + taken[2 * ROWS :]


def gone_from(lhot):
    ones = jnp.ones((8, lhot.shape[0]), BF16)
    return jnp.dot(ones, lhot, preferred_element_type=F32)[0:1]


def packs_of(taken, lists, section, span, slots):
    width = lists.shape[-1]
    packs = []
    for d in range(2):
        valid = lists[0, 0, section, d : d + 1, :] < slots
        pack = taken[:, d * width : (d + 1) * width]
        cell = pack[HOST : HOST + 1].astype(jnp.int32) % span
        cell = jnp.where(valid, cell.astype(F32), -1.0)
        row = iota(pack.shape, 0)
        pack = jnp.where(row == HOST, cell, jnp.where(valid & (row < HOST), pack, 0.0))
        packs.append(pack)
    left, right = packs
    flip = odd("azim") == 1
    return jnp.where(flip, left, right), jnp.where(flip, right, left)


def rows_kernel(gas, after, near, far):
    send_rows(gas, near, far)


def send_rows(gas, near, far):
    cr = gas.shape[2]
    flip = odd("radax") == 1
    for f in range(gas.shape[0]):
        low, high = gas[f, :, 0, :], gas[f, :, cr - 1, :]
        near[f] = jnp.where(flip, low, high)
        far[f] = jnp.where(flip, high, low)


def probe_one_kernel(
    count, gas, transport, chemistry, evap, source_map, lists, mass, state, host_in,
    parcels, on, off, table, hots, source, used, cells, probed, lhot,
):
    nf, ca, cr, cz = gas.shape
    slots = probed.shape[1]
    fill_table(table, transport, chemistry, evap, source_map)
    host = host_in[0]
    used[...] = jnp.broadcast_to(count[...].astype(F32), used.shape)
    live = (iota((1, slots), 1) < count[...]).astype(F32)
    attr = jnp.concatenate([mass[0]] + [state[k, 0] for k in range(state.shape[0])], axis=0)
    source[:nf] = parcel_work(gas, host, attr, live, table, parcels, cells, hots, probed)
    list_hots(lists, 0, slots, lhot)
    on[...], off[...] = packs_of(gather(parcels[:, :slots], lhot[...]), lists, 0, cr * cz, slots)
    parcels[LIVE : LIVE + 1, :slots] = jnp.where(gone_from(lhot[...]) > 0.5, 0.0, live)


def field_one_kernel(reach, gas, table, parcels, hots, source, out, total, tanh):
    nf, ca, cr, cz = gas.shape
    host = parcels[HOST : HOST + 1, :reach].astype(jnp.int32)
    deposit_all(source, host, hots, gas.shape, reach, total)
    for f, a, terms in inner_terms(gas, table, tanh, (0, ca - 1)):
        terms += total[f * cr : (f + 1) * cr, a * cz : (a + 1) * cz]
        out[f, min(a, 1)] = gas[f, a] + DT * terms


def radial_halos(near, far, f):
    block = lax.axis_index("radax")
    flip = odd("radax") == 1
    north = jnp.where(flip, far[f], near[f])
    south = jnp.where(flip, near[f], far[f])
    return jnp.where(block == 0, 0.0, south), jnp.where(block == lax.axis_size("radax") - 1, 0.0, north)


def edge_kernel(table, outer, far, near, pack_on, pack_off, send_on, send_off):
    nf, _, cr, cz = outer.shape
    ca = near.shape[1]
    flip = odd("azim") == 1
    row = iota((cr, cz), 0)
    for f in range(nf):
        south, north = radial_halos(near, far, f)
        nu = DT * spread(table, NU, f, cr)
        low, high = (
            outer[f, k]
            + nu
            * (
                jnp.where(row == 0, jnp.broadcast_to(south[a : a + 1], (cr, cz)), 0.0)
                + jnp.where(row == cr - 1, jnp.broadcast_to(north[a : a + 1], (cr, cz)), 0.0)
            )
            for k, a in ((0, 0), (1, ca - 1))
        )
        send_on[f * cr : (f + 1) * cr] = jnp.where(flip, low, high)
        send_off[f * cr : (f + 1) * cr] = jnp.where(flip, high, low)
    send_on[nf * cr :] = pack_on[...]
    send_off[nf * cr :] = pack_off[...]


def join_kernel(gas, table, outer, total, off, on, far, near, out, tanh):
    nf, ca, cr, cz = gas.shape
    for f in range(nf):
        out[f, 0] = outer[f, 0]
        out[f, ca - 1] = outer[f, 1]
    for f, a, terms in inner_terms(gas, table, tanh, range(1, ca - 1)):
        terms += total[f * cr : (f + 1) * cr, a * cz : (a + 1) * cz]
        out[f, a] = gas[f, a] + DT * terms
    for f in range(nf):
        west, east = sides(on[f * cr : (f + 1) * cr], off[f * cr : (f + 1) * cr])
        edge_terms(DT, table, out, f, west, east, near, far)


def probe_two_kernel(
    gas, table, lists, old, near, far, parcels, hots, source, taken, lhot, cells, probed
):
    slots = probed.shape[1]
    send_rows(gas, near, far)
    host = old[HOST : HOST + 1, :slots].astype(jnp.int32)
    live = old[LIVE : LIVE + 1, :slots]
    source[: gas.shape[0]] = parcel_work(
        gas, host, old[0:HOST, :slots], live, table, parcels, cells, hots, probed
    )
    list_hots(lists, 1, slots, lhot)
    taken[...] = gather(parcels[:, :slots], lhot[...])
    parcels[GONE : GONE + 1, :slots] = gone_from(lhot[...])


def field_two_kernel(reach, gas, table, old_gas, parcels, hots, source, out, total, tanh):
    nf, ca, cr, cz = gas.shape
    host = parcels[HOST : HOST + 1, :reach].astype(jnp.int32)
    deposit_all(source, host, hots, gas.shape, reach, total)
    for f, a, terms in inner_terms(gas, table, tanh, range(ca - 1)):
        terms += total[f * cr : (f + 1) * cr, a * cz : (a + 1) * cz]
        out[f, a] = 0.5 * (old_gas[f, a] + gas[f, a] + DT * terms)
    for f in range(nf):
        out[f, ca - 1] = total[f * cr : (f + 1) * cr, (ca - 1) * cz :]


def parcel_work(gas, host, attr, live, table, parcels, cells, hots, probed):
    slots = probed.shape[1]
    probe_all(gas, host, cells, hots, probed)
    rows, source = react(probed[...], attr, live, table, gas.shape[0])
    parcels[...] = jnp.zeros_like(parcels)
    parcels[0:ROWS, :slots] = jnp.concatenate(
        rows + [host.astype(F32), live, jnp.zeros((ROWS - LIVE - 1, slots), F32)], axis=0
    )
    return source


def edge_terms(scale, table, out, f, west, east, near, far):
    ca, cr = out.shape[1], out.shape[2]
    out[f, 0] += (scale * spread(table, WEST, f, cr)) * west
    out[f, ca - 1] += (scale * spread(table, EAST, f, cr)) * east
    south, north = radial_halos(near, far, f)
    nu = scale * spread(table, NU, f, ca)
    out[f, :, 0, :] += nu * south
    out[f, :, cr - 1, :] += nu * north


def put(parcels, pack, start, live):
    width = pack.shape[1]
    row = iota(pack.shape, 0)
    pack = jnp.where(row == LIVE, live, pack)
    shift = start % width
    first = pl.multiple_of((start // width) * width, width)
    pack = pltpu.roll(pack, shift, 1)
    lane = iota(pack.shape, 1)
    taken = pack[LIVE : LIVE + 1] > 0.5
    here = parcels[:, pl.ds(first, width)]
    parcels[:, pl.ds(first, width)] = jnp.where(taken & (lane >= shift) & (row != GONE), pack, here)
    second = pl.multiple_of(first + width, width)
    here = parcels[:, pl.ds(second, width)]
    parcels[:, pl.ds(second, width)] = jnp.where(taken & (lane < shift) & (row != GONE), pack, here)


def sides(on, off):
    flip = odd("azim") == 1
    return jnp.where(flip, on, off), jnp.where(flip, off, on)


def scalar(ref):
    return jnp.max(ref[0:1]).astype(jnp.int32)


def arrive_kernel(
    count, gas, table, lists, on, off, old, taken, lhot, parcels, send_on, send_off, sources, used, cells
):
    nf, ca, cr, cz = gas.shape
    slots = lhot.shape[1]
    base = nf * cr
    packs = sides(on[base:], off[base:])
    parcels[...] = old[...]
    start = scalar(count)
    for side in range(2):
        layer = side * (ca - 1)
        pack = packs[side]
        cell = pack[HOST : HOST + 1].astype(jnp.int32)
        live = (cell >= 0).astype(F32)
        for f in range(nf):
            upper, lower = parts_of(gas[f, layer], 2)
            cells[f * cr : (f + 1) * cr, :cz] = upper
            cells[f * cr : (f + 1) * cr, cz:] = lower
        zhot = hot(iota((cz, cell.shape[1]), 0) == cell % cz)
        found = jnp.dot(cells[:, :cz], zhot, preferred_element_type=F32)
        found += jnp.dot(cells[:, cz:], zhot, preferred_element_type=F32)
        mask = iota((cr, cell.shape[1]), 0) == cell // cz
        found = jnp.where(mask[None], found.reshape(nf, cr, cell.shape[1]), 0.0)
        probed = jnp.sum(found, axis=1)
        rows, source = react(probed, pack[0:HOST], live, table, nf)
        sources[side, :nf] = source
        sources[side, nf : nf + 1] = pack[HOST : HOST + 1]
        home = (cell + layer * cr * cz).astype(F32)
        moved = jnp.concatenate(rows + [home, live, jnp.zeros((ROWS - LIVE - 1, cell.shape[1]), F32)], 0)
        put(parcels, moved, start, live)
        start = start + jnp.sum(live).astype(jnp.int32)
    used[...] = jnp.broadcast_to(start.astype(F32), used.shape)
    width = lists.shape[-1]
    first = pl.multiple_of(scalar(count), width)
    window = pl.ds(first, 2 * width)
    again = gather(parcels[:, window], lhot[:, window])
    names = jnp.concatenate([lists[0, 0, 1, d : d + 1, :] for d in range(2)], axis=1)
    inside = (names >= first) & (names < first + 2 * width)
    both = jnp.where(inside, again, taken[...])
    send_on[...], send_off[...] = packs_of(both, lists, 1, cr * cz, slots)
    gone = parcels[GONE : GONE + 1, :slots] > 0.5
    parcels[LIVE : LIVE + 1, :slots] = jnp.where(gone, 0.0, parcels[LIVE : LIVE + 1, :slots])


def finish_kernel(table, base, gas, off, on, near, far, sources, middle, out, tanh):
    nf, ca, cr, cz = out.shape
    out[:, : ca - 1] = base[:, : ca - 1]
    for f, a, terms in inner_terms(middle, table, tanh, (ca - 1,)):
        out[f, a] = 0.5 * (gas[f, a] + middle[f, a] + DT * (terms + base[f, a]))
    for f in range(nf):
        west, east = sides(on[f * cr : (f + 1) * cr], off[f * cr : (f + 1) * cr])
        west += (DT * spread(table, EAST, f, cr)) * gas[f, 0]
        east += (DT * spread(table, WEST, f, cr)) * gas[f, ca - 1]
        edge_terms(0.5 * DT, table, out, f, west, east, near, far)
    for side in range(2):
        layer = side * (ca - 1)
        cell = sources[side, nf : nf + 1].astype(jnp.int32)
        mask = iota((cr, cell.shape[1]), 0) == cell // cz
        laid = jnp.where(mask[None], sources[side, :nf][:, None, :], 0.0)
        upper, lower = parts_of(laid.reshape(nf * cr, cell.shape[1]), 2)
        zhot = hot(iota((cz, cell.shape[1]), 0) == cell % cz)
        total = across(upper, zhot) + across(lower, zhot)
        for f in range(nf):
            out[f, layer] += (0.5 * DT) * total[f * cr : (f + 1) * cr]


def place_kernel(far_offset, count, off, on, old, mass, state, host, used, parcels):
    slots = mass.shape[-1]
    parcels[...] = old[...]
    packs = sides(on[...], off[...])
    start = scalar(count)
    for side in range(2):
        pack = packs[side]
        live = (pack[HOST : HOST + 1] >= 0.0).astype(F32)
        row = iota(pack.shape, 0)
        pack = jnp.where(row == HOST, pack + float(side * far_offset), pack)
        put(parcels, pack, start, live)
        start = start + jnp.sum(live).astype(jnp.int32)
    used[...] = jnp.broadcast_to(start, (1, 1))
    live = parcels[LIVE : LIVE + 1, :slots] > 0.5
    mass[0] = jnp.where(live, parcels[0:1, :slots], 0.0)
    for k in range(state.shape[0]):
        state[k, 0] = jnp.where(live, parcels[k + 1 : k + 2, :slots], 0.0)
    host[0] = jnp.where(live, parcels[HOST : HOST + 1, :slots].astype(jnp.int32), -1)


def swap(array, axis, phase):
    size = lax.axis_size(axis)
    pairs = []
    for i in range(phase, size + phase, 2):
        j = (i + 1) % size
        pairs += [(i, j), (j, i)]
    return lax.ppermute(array, axis, pairs)


def swap_rows(array, phase):
    sectors, blocks = lax.axis_size("azim"), lax.axis_size("radax")
    pairs = []
    for i in range(sectors):
        for j in range(blocks):
            other = j + 1 if (j - phase) % 2 == 0 else j - 1
            target = (i, other) if 0 <= other < blocks else (i ^ 1, j)
            pairs.append((i * blocks + j, target[0] * blocks + target[1]))
    return lax.ppermute(array, ("azim", "radax"), pairs)


def on_device(
    gas, transport, chemistry, evap, source_map, mass, state, host, count, crossing
):
    nf, ca, cr, cz = gas.shape
    slots = mass.shape[-1]
    width = crossing.shape[-1]
    padded = slots + 2 * width
    ring, pack = shape((nf, ca, cz)), shape((ROWS, width))
    tile = shape((8, LANES))
    grid, slotted = shape(gas.shape), shape((ROWS, padded))
    evap, source_map = evap.reshape(1, nf), source_map.T
    off, on = call(
        pack_kernel,
        [shape((nf, cr, cz)), shape((nf, cr, cz))],
        [HBM],
        [VMEM] * 2,
        (pltpu.with_memory_space_constraint(gas, pltpu.HBM),),
        scratch=[pltpu.SemaphoreType.DMA((2,))],
        flops=5_000_000_000,
        moved=2_000_000,
    )
    packed = off
    off = swap(off.reshape(nf * cr, cz), "azim", 1)
    on = swap(on.reshape(nf * cr, cz), "azim", 0)

    near, far = call(rows_kernel, [ring, ring], [VMEM] * 2, [VMEM] * 2, (gas, packed), moved=100_000)
    near = swap_rows(near, 0)
    far = swap_rows(far, 1)
    hots, lhot = shape((ca * cz, slots), BF16), shape((2 * width, slots), BF16)
    source = shape((ROWS, slots))
    probe_scratch = [pltpu.VMEM((nf * cr, 2 * ca * cz), BF16), pltpu.VMEM((ROWS, slots), F32)]
    tanh_scratch = pltpu.VMEM(gas.shape, F32)
    total = shape((nf * cr, ca * cz))
    heavy = dict(flops=3_000_000_000, moved=2_000_000, trans=300_000)
    light = dict(flops=1_000_000, moved=10_000)
    parcels, pack_on, pack_off, table, cell_hots, sources, used = call(
        probe_one_kernel,
        [slotted, pack, pack, shape((SOURCE + source_map.shape[0] + nf, ROWS, LANES)), hots, source, tile],
        [VMEM] * 10,
        [VMEM] * 7,
        (count, gas, transport, chemistry, evap, source_map, crossing, mass, state, host),
        scratch=probe_scratch + [pltpu.VMEM(lhot.shape, BF16)],
        **heavy,
    )
    outer, total = call(
        functools.partial(field_one_kernel, slots - 4 * width),
        [shape((nf, 2, cr, cz)), total],
        [VMEM] * 5,
        [VMEM] * 2,
        (gas, table, parcels, cell_hots, sources),
        scratch=[tanh_scratch],
        **light,
    )
    longer = shape((nf * cr + ROWS, cz))
    send_on, send_off = call(
        edge_kernel,
        [longer, longer],
        [VMEM] * 6,
        [VMEM] * 2,
        (table, outer, far, near, pack_on, pack_off),
        **light,
    )
    section_one = call(
        join_kernel,
        grid,
        [VMEM] * 8,
        VMEM,
        (gas, table, outer, total, off, on, far, near),
        scratch=[tanh_scratch],
        **heavy,
    )
    off = swap(send_off, "azim", 1)
    on = swap(send_on, "azim", 0)
    near, far, parcels, cell_hots, sources, taken, named = call(
        probe_two_kernel,
        [ring, ring, slotted, hots, source, shape((ROWS, 2 * width)), lhot],
        [VMEM] * 4,
        [VMEM] * 7,
        (section_one, table, crossing, parcels),
        scratch=probe_scratch,
        **light,
    )
    near = swap_rows(near, 0)
    far = swap_rows(far, 1)
    base = call(
        functools.partial(field_two_kernel, slots - 4 * width),
        grid,
        [VMEM] * 6,
        VMEM,
        (section_one, table, gas, parcels, cell_hots, sources),
        scratch=[pltpu.VMEM(total.shape, F32), tanh_scratch],
        **light,
    )
    parcels, pack_on, pack_off, sources, used_now = call(
        arrive_kernel,
        [slotted, pack, pack, shape((2, ROWS, width)), tile],
        [VMEM] * 9,
        [VMEM] * 5,
        (used, section_one, table, crossing, on, off, parcels, taken, named),
        scratch=[pltpu.VMEM((nf * cr, 2 * cz), BF16)],
        flops=100_000_000,
        moved=2_000_000,
    )
    pack_off = swap(pack_off, "azim", 1)
    pack_on = swap(pack_on, "azim", 0)
    gas_next = call(
        finish_kernel,
        shape(gas.shape),
        [VMEM] * 9,
        VMEM,
        (table, base, gas, off, on, near, far, sources, section_one),
        scratch=[tanh_scratch],
        flops=100_000_000,
        moved=3_000_000,
    )
    mass_next, state_next, host_next, count_next = call(
        functools.partial(place_kernel, (ca - 1) * cr * cz),
        [shape(mass.shape), shape(state.shape), shape(host.shape, jnp.int32), shape((1, 1), jnp.int32)],
        [VMEM] * 4,
        [VMEM] * 4,
        (used_now, pack_off, pack_on, parcels),
        scratch=[pltpu.VMEM((ROWS, padded), F32)],
        moved=500_000,
    )
    return gas_next, mass_next, state_next, host_next, count_next


def solution(mesh):
    in_specs = (
        P(None, "azim", "radax", None),
        P(),
        P(),
        P(),
        P(),
        P("azim", "radax", None),
        P(None, "azim", "radax", None),
        P("azim", "radax", None),
        P("azim", "radax"),
        P("azim", "radax", None, None, None),
    )
    out_specs = (
        P(None, "azim", "radax", None),
        P("azim", "radax", None),
        P(None, "azim", "radax", None),
        P("azim", "radax", None),
        P("azim", "radax"),
    )
    return jax.shard_map(
        on_device, mesh=mesh, in_specs=in_specs, out_specs=out_specs, check_vma=False
    )
```
